128 devices in a mesh: mp: 4 (over y_lo, core), latent: 32 (over y_hi, x, z).
Axes of the slice: x: 4, y: 4 (y_hi: 2, y_lo: 2; y = y_hi * 2 + y_lo), z: 4, core: 2. Of those that a mesh axis runs over, the one named last changes fastest.
Arguments:
- resid_clean: bfloat16 [128, 4608], P(('mp', 'latent')), may hold values from -6 to 6
- resid_corrupt: bfloat16 [128, 4608], P(('mp', 'latent')), may hold values from -6 to 6
- answer_ids: int32 [128, 2], replicated, may hold values from 0 to 127, all different within a row
- unembed: bfloat16 [128, 4608], replicated, may hold values from -1.5 to 1.5
- pre_gain: float32 [4608], replicated, may hold values from 0.25 to 1.75
- post_gain: float32 [4608], replicated, may hold values from 0.25 to 1.75
- final_gain: float32 [4608], replicated, may hold values from 0.25 to 1.75
- w_gate: bfloat16 [4608, 36864], P(None, ('mp', 'latent')), may hold values from -0.09375 to 0.09375
- w_up: bfloat16 [4608, 36864], P(None, ('mp', 'latent')), may hold values from -0.09375 to 0.09375
- w_down: bfloat16 [36864, 4608], P(('mp', 'latent')), may hold values from -0.03125 to 0.03125
- w_enc: bfloat16 [4608, 65536], P(None, ('mp', 'latent')), may hold values from -0.09375 to 0.09375
- b_enc: float32 [65536], P(('mp', 'latent')), may hold values from -3 to 3
- w_dec: bfloat16 [65536, 4608], P(('mp', 'latent')), may hold values from -0.09375 to 0.09375
Outputs:
- attribution: float32 [1, 65536], P(None, ('mp', 'latent'))
The draws below stay inside these ranges and needn't reach their ends.
Inputs may be any that keep to these rules, and one draw needn't show every extreme that they name: `answer_ids`: the two indices of a token differ.
All inputs are finite; a program needn't handle non-finite values.
Results may differ from the reference program's by a relative error of at most 0.0056.
Values may be sent and summed in bfloat16 or wider, within the bound.
No kernel may reach another device: no remote copies, remote signals or barrier semaphores. Data moves between devices by JAX's collectives and lax.ppermute only.
A program may use at most 128 MiB of HBM per device.

```python
import jax
import jax.numpy as jnp
from jax import lax

D = 4608
FF = 36864
LATENTS = 65536
CANDS = 128
SEQ = 128
PAIRS = 1
TOK = 128


def block_levels(stream_key, extent, cuts, low, largest):
    def one(position, parts):
        heights = jax.random.uniform(jax.random.fold_in(jax.random.fold_in(stream_key, 6), position), (parts,), jnp.float32, low / len(cuts), largest / len(cuts))
        return jnp.repeat(jnp.exp(heights), extent[position] // parts).reshape((-1,) + (1,) * (len(extent) - position - 1))

    gain = one(*cuts[0])
    for cut in cuts[1:]:
        gain = gain * one(*cut)
    return gain


def distinct(own_key, rows, number_of, top, lift):
    ranking = jax.random.permutation(jax.random.fold_in(own_key, 1), number_of)
    boost = ranking
    for power in range(3):
        boost = boost * boost // number_of
    boost = boost * lift // number_of
    chance = jax.random.randint(jax.random.fold_in(own_key, 2), (rows, number_of), 0, 4096) + boost
    sure = jax.random.permutation(jax.random.fold_in(own_key, 3), rows)[jnp.arange(number_of) % rows]
    chance = jnp.where(jnp.arange(rows)[:, None] == sure[None, :], 1 << 14, chance)
    score = chance * number_of + jnp.arange(number_of)
    return lax.top_k(score.astype(jnp.int32), top)[1].astype(jnp.int32)


def noise(own_key, extent, spread, bound, split=(), kind=jnp.bfloat16):
    level = block_levels(own_key, extent, split, -0.22, 0.18) if split else 1.0
    values = jax.random.normal(own_key, extent, jnp.float32) * spread * level
    return jnp.minimum(jnp.maximum(values, -bound), bound).astype(kind)


def setup_inputs(seed: int = 0) -> dict:
    keys = jax.random.split(jax.random.key(seed), 14)
    resid_clean = noise(keys[0], (TOK, D), 1.0, 6.0, ((0, 128),))
    resid_corrupt = noise(keys[1], (TOK, D), 1.0, 6.0, ((0, 128),))
    answer_ids = distinct(keys[2], TOK, CANDS, 2, 0)
    unembed = noise(keys[3], (CANDS, D), 0.25, 1.5)
    pre_gain = jnp.clip(1.0 + 0.15 * jax.random.normal(keys[4], (D,), jnp.float32), 0.25, 1.75)
    post_gain = jnp.clip(1.0 + 0.15 * jax.random.normal(keys[5], (D,), jnp.float32), 0.25, 1.75)
    final_gain = jnp.clip(1.0 + 0.15 * jax.random.normal(keys[6], (D,), jnp.float32), 0.25, 1.75)
    w_gate = noise(keys[7], (D, FF), D ** -0.5, 0.09375, ((1, 128),))
    w_up = noise(keys[8], (D, FF), D ** -0.5, 0.09375, ((1, 128),))
    w_down = noise(keys[9], (FF, D), FF ** -0.5, 0.03125, ((0, 128),))
    w_enc = noise(keys[10], (D, LATENTS), D ** -0.5, 0.09375, ((1, 128),))
    b_enc = noise(keys[11], (LATENTS,), 0.5, 3.0, ((0, 128),), jnp.float32)
    w_dec = noise(keys[12], (LATENTS, D), D ** -0.5, 0.09375, ((0, 128),))
    return {"resid_clean": resid_clean, "resid_corrupt": resid_corrupt, "answer_ids": answer_ids, "unembed": unembed, "pre_gain": pre_gain, "post_gain": post_gain, "final_gain": final_gain, "w_gate": w_gate, "w_up": w_up, "w_down": w_down, "w_enc": w_enc, "b_enc": b_enc, "w_dec": w_dec}


epsilon = 1e-06
gelu_scale = 0.7978845608028654
gelu_cubic = 0.044715

def gelu_tanh(value):
    return 0.5 * value * (1.0 + jnp.tanh(gelu_scale * (value + gelu_cubic * value * value * value)))

def gelu_slope(value):
    inner = jnp.tanh(gelu_scale * (value + gelu_cubic * value * value * value))
    return 0.5 * (1.0 + inner) + 0.5 * value * (1.0 - inner * inner) * gelu_scale * (1.0 + 3.0 * gelu_cubic * value * value)

def contract_last(left, right):
    return lax.dot_general(left, right, (((1,), (1,)), ((), ())), preferred_element_type=jnp.float32)

def output_grads(stream, mlp_out, answers, unembed, post_gain, final_gain):
    inv_post = lax.rsqrt(lax.optimization_barrier(jnp.mean(mlp_out * mlp_out, axis=-1, keepdims=True)) + epsilon)
    output = stream + mlp_out * inv_post * post_gain
    inv_final = lax.rsqrt(lax.optimization_barrier(jnp.mean(output * output, axis=-1, keepdims=True)) + epsilon)
    candidate = lax.broadcasted_iota(jnp.int32, (answers.shape[0], unembed.shape[0]), 1)
    selector = ((candidate == answers[:, 0:1]).astype(jnp.float32) - (candidate == answers[:, 1:2]).astype(jnp.float32)).astype(jnp.bfloat16)
    direction = jnp.dot(selector, unembed, preferred_element_type=jnp.float32)
    weighted = final_gain * direction
    grad_output = inv_final * weighted - output * (inv_final * inv_final * inv_final) * lax.optimization_barrier(jnp.mean(weighted * output, axis=-1, keepdims=True))
    post_grad = post_gain * grad_output
    grad_mlp = (inv_post * post_grad - mlp_out * (inv_post * inv_post * inv_post) * lax.optimization_barrier(jnp.mean(post_grad * mlp_out, axis=-1, keepdims=True))).astype(jnp.bfloat16)
    return (grad_output, grad_mlp)

def reference(resid_clean, resid_corrupt, answer_ids, unembed, pre_gain, post_gain, final_gain, w_gate, w_up, w_down, w_enc, b_enc, w_dec):
    stream = resid_clean.astype(jnp.float32)
    inv_pre = lax.rsqrt(lax.optimization_barrier(jnp.mean(stream * stream, axis=-1, keepdims=True)) + epsilon)
    normed = (stream * inv_pre * pre_gain).astype(jnp.bfloat16)
    gate_pre = jnp.dot(normed, w_gate, preferred_element_type=jnp.float32)
    up_proj = jnp.dot(normed, w_up, preferred_element_type=jnp.float32)
    activated = gelu_tanh(gate_pre)
    hidden = (activated * up_proj).astype(jnp.bfloat16)
    mlp_out = jnp.dot(hidden, w_down, preferred_element_type=jnp.float32)
    grad_output, grad_mlp = output_grads(stream, mlp_out, answer_ids, unembed, post_gain, final_gain)
    grad_hidden = contract_last(grad_mlp, w_down)
    grad_gate = (grad_hidden * up_proj * gelu_slope(gate_pre)).astype(jnp.bfloat16)
    grad_up = (grad_hidden * activated).astype(jnp.bfloat16)
    grad_normed = contract_last(grad_gate, w_gate) + contract_last(grad_up, w_up)
    pre_grad = pre_gain * grad_normed
    grad_stream = (grad_output + inv_pre * pre_grad - stream * (inv_pre * inv_pre * inv_pre) * lax.optimization_barrier(jnp.mean(pre_grad * stream, axis=-1, keepdims=True))).astype(jnp.bfloat16)
    clean_code = jax.nn.relu(jnp.dot(resid_clean, w_enc, preferred_element_type=jnp.float32) + b_enc)
    corrupt_code = jax.nn.relu(jnp.dot(resid_corrupt, w_enc, preferred_element_type=jnp.float32) + b_enc)
    change = clean_code - corrupt_code
    projected = contract_last(grad_stream, w_dec)
    product = change * projected
    return lax.optimization_barrier(jnp.sum(product.reshape(PAIRS, SEQ, LATENTS), axis=1))
```

```python
import jax
import jax.numpy as jnp
from jax import lax
from jax.sharding import Mesh
from jax.sharding import PartitionSpec as P

epsilon = 1e-06
gelu_scale = 0.7978845608028654
gelu_cubic = 0.044715

DEVICES = ("y_lo", "core", "y_hi", "x", "z")
CHIPS = ("y_lo", "y_hi", "x", "z")
SWAP = [(0, 1), (1, 0)]
F32 = jnp.float32
BF16 = jnp.bfloat16


def gelu_tanh(value):
    return 0.5 * value * (1.0 + jnp.tanh(gelu_scale * (value + gelu_cubic * value * value * value)))


def gelu_slope(value):
    inner = jnp.tanh(gelu_scale * (value + gelu_cubic * value * value * value))
    return 0.5 * (1.0 + inner) + 0.5 * value * (1.0 - inner * inner) * gelu_scale * (
        1.0 + 3.0 * gelu_cubic * value * value
    )


def contract_last(left, right):
    return lax.dot_general(
        left, right, (((1,), (1,)), ((), ())), preferred_element_type=jnp.float32
    )


def mean_row(value):
    return jnp.mean(value, axis=-1, keepdims=True)


def gathered(row):
    chips = lax.axis_size(CHIPS)
    same = lax.all_to_all(
        jnp.broadcast_to(row, (chips, row.shape[1])), CHIPS, 0, 0, tiled=True
    )
    other = lax.ppermute(same, "core", SWAP)
    return jnp.concatenate([same, other], axis=0)


def summed_at_owner(partial):
    half = partial.shape[0] // 2
    arrived = lax.ppermute(partial[half:].astype(BF16), "core", SWAP)
    chip_sum = (partial[:half] + arrived.astype(F32)).astype(BF16)
    pieces = lax.all_to_all(chip_sum, CHIPS, 0, 0, tiled=True)
    return jnp.sum(pieces.astype(F32), axis=0, keepdims=True)


def local(
    resid_clean,
    resid_corrupt,
    answer_ids,
    unembed,
    pre_gain,
    post_gain,
    final_gain,
    w_gate,
    w_up,
    w_down,
    w_enc,
    b_enc,
    w_dec,
):
    token = lax.axis_index(DEVICES)
    answers = lax.dynamic_slice_in_dim(answer_ids, token, 1, 0)
    direction = lax.dynamic_slice_in_dim(unembed, answers[0, 0], 1, 0).astype(
        F32
    ) - lax.dynamic_slice_in_dim(unembed, answers[0, 1], 1, 0).astype(F32)
    own = resid_clean.astype(F32)
    own_inv = lax.rsqrt(mean_row(own * own) + epsilon)

    clean_all = gathered(resid_clean)
    stream = clean_all.astype(F32)
    inv_pre = lax.rsqrt(mean_row(stream * stream) + epsilon)
    normed = (stream * inv_pre * pre_gain).astype(BF16)
    gate_pre = jnp.dot(normed, w_gate, preferred_element_type=F32)
    up_proj = jnp.dot(normed, w_up, preferred_element_type=F32)
    activated = gelu_tanh(gate_pre)
    hidden = (activated * up_proj).astype(BF16)
    mlp_out = summed_at_owner(jnp.dot(hidden, w_down, preferred_element_type=F32))

    inv_post = lax.rsqrt(mean_row(mlp_out * mlp_out) + epsilon)
    output = own + mlp_out * inv_post * post_gain
    inv_final = lax.rsqrt(mean_row(output * output) + epsilon)
    weighted = final_gain * direction
    grad_output = inv_final * weighted - output * (inv_final * inv_final * inv_final) * mean_row(
        weighted * output
    )
    post_grad = post_gain * grad_output
    grad_mlp = (
        inv_post * post_grad
        - mlp_out * (inv_post * inv_post * inv_post) * mean_row(post_grad * mlp_out)
    ).astype(BF16)

    grad_mlp_all = gathered(grad_mlp)
    grad_hidden = contract_last(grad_mlp_all, w_down)
    grad_gate = (grad_hidden * up_proj * gelu_slope(gate_pre)).astype(BF16)
    grad_up = (grad_hidden * activated).astype(BF16)
    grad_normed = summed_at_owner(
        contract_last(grad_gate, w_gate) + contract_last(grad_up, w_up)
    )
    pre_grad = pre_gain * grad_normed
    grad_stream = (
        grad_output
        + own_inv * pre_grad
        - own * (own_inv * own_inv * own_inv) * mean_row(pre_grad * own)
    ).astype(BF16)

    corrupt_all = gathered(resid_corrupt)
    clean_code = jax.nn.relu(jnp.dot(clean_all, w_enc, preferred_element_type=F32) + b_enc)
    corrupt_code = jax.nn.relu(jnp.dot(corrupt_all, w_enc, preferred_element_type=F32) + b_enc)
    change = clean_code - corrupt_code
    projected = contract_last(gathered(grad_stream), w_dec)
    return jnp.sum(change * projected, axis=0, keepdims=True)


def solution(mesh):
    fine = Mesh(mesh.devices.reshape(2, 2, 2, 4, 4), DEVICES)
    return jax.shard_map(
        local,
        mesh=fine,
        in_specs=(
            P(DEVICES, None),
            P(DEVICES, None),
            P(),
            P(),
            P(),
            P(),
            P(),
            P(None, DEVICES),
            P(None, DEVICES),
            P(DEVICES, None),
            P(None, DEVICES),
            P(DEVICES),
            P(DEVICES, None),
        ),
        out_specs=P(None, DEVICES),
        check_vma=False,
    )
```

```python
import jax
import jax.numpy as jnp
from jax import lax
from jax.experimental import pallas as pl
from jax.experimental.pallas import tpu as pltpu
from jax.sharding import Mesh
from jax.sharding import PartitionSpec as P

epsilon = 1e-06
gelu_scale = 0.7978845608028654
gelu_cubic = 0.044715

DEVICES = ("y_lo", "core", "y_hi", "x", "z")
COLUMN = ("y_lo", "core", "y_hi")
PLANE = ("x", "z")
SWAP = [(0, 1), (1, 0)]
F32 = jnp.float32
BF16 = jnp.bfloat16
VMEM = pl.BlockSpec(memory_space=pltpu.VMEM)
SMEM = pl.BlockSpec(memory_space=pltpu.SMEM)


def shape(dims, dtype):
    return jax.ShapeDtypeStruct(dims, dtype)


def call(kernel, outs, *args, scratch=()):
    specs = [SMEM if a.dtype == jnp.int32 else VMEM for a in args]
    return pl.pallas_call(
        kernel,
        out_shape=outs,
        in_specs=specs,
        out_specs=jax.tree.map(lambda _: VMEM, outs),
        scratch_shapes=scratch,
        compiler_params=pltpu.CompilerParams(vmem_limit_bytes=56 << 20),
    )(*args)


def gelu_tanh(value):
    return 0.5 * value * (1.0 + jnp.tanh(gelu_scale * (value + gelu_cubic * value * value * value)))


def gelu_slope(value):
    inner = jnp.tanh(gelu_scale * (value + gelu_cubic * value * value * value))
    return 0.5 * (1.0 + inner) + 0.5 * value * (1.0 - inner * inner) * gelu_scale * (
        1.0 + 3.0 * gelu_cubic * value * value
    )


def dot_nn(left, right):
    return jnp.dot(left, right, preferred_element_type=F32)


def dot_nt(left, right):
    return lax.dot_general(left, right, (((1,), (1,)), ((), ())), preferred_element_type=F32)


def mean_row(value):
    return jnp.mean(value, axis=-1, keepdims=True)


def halves(core_ref, width):
    core = core_ref[0]
    return (
        pl.ds(pl.multiple_of(core * width, 128), width),
        pl.ds(pl.multiple_of((1 - core) * width, 128), width),
    )


def forward_kernel(core, own, other, w_gate, w_up, w_down, gain, send, hidden, gate, up, normed):
    width = own.shape[1]
    mine, theirs = halves(core, width)
    a, b = own[...].astype(F32), other[...].astype(F32)
    total = jnp.sum(a * a, axis=-1, keepdims=True) + jnp.sum(b * b, axis=-1, keepdims=True)
    inv = lax.rsqrt(total / (2 * width) + epsilon)
    normed[:, mine] = (a * inv * gain[:, mine]).astype(BF16)
    normed[:, theirs] = (b * inv * gain[:, theirs]).astype(BF16)
    gate_pre = dot_nt(normed[...], w_gate[...])
    up_proj = dot_nt(normed[...], w_up[...])
    gate[...] = gate_pre
    up[...] = up_proj
    act = (gelu_tanh(gate_pre) * up_proj).astype(BF16)
    hidden[...] = act
    send[...] = dot_nn(act, w_down[:, theirs]).astype(BF16)


def forward_sum_kernel(core, hidden, w_down, arrived, out):
    mine, _ = halves(core, arrived.shape[1])
    total = dot_nn(hidden[...], w_down[:, mine]) + arrived[...].astype(F32)
    out[...] = total.astype(BF16).reshape(out.shape)


def plane_sum_kernel(pieces, out):
    total = jnp.sum(pieces[...].astype(F32), axis=0).astype(BF16)
    for peer in range(out.shape[0]):
        out[peer] = total


def column_total(pieces):
    sums = []
    for core in range(2):
        total = None
        for peer in range(pieces.shape[0]):
            if (peer // 2) % 2 == core:
                part = pieces[peer].astype(F32)
                total = part if total is None else total + part
        sums.append(total)
    return jnp.concatenate(sums, axis=1)


def direction_kernel(answers, unembed, gain, out):
    lanes = lax.broadcasted_iota(jnp.int32, (1, unembed.shape[0]), 1)
    rows = []
    for token in range(out.shape[0]):
        rows.append(
            (lanes == answers[token, 0]).astype(F32) - (lanes == answers[token, 1]).astype(F32)
        )
    selector = jnp.concatenate(rows, axis=0).astype(BF16)
    out[...] = gain[...] * dot_nn(selector, unembed[...])


def output_kernel(core, pieces, stream, weighted, post_gain, out, grad_output, grad_mlp):
    mine, _ = halves(core, out.shape[2])
    mlp_out = column_total(pieces)
    inv_post = lax.rsqrt(mean_row(mlp_out * mlp_out) + epsilon)
    output = stream[...].astype(F32) + mlp_out * inv_post * post_gain[...]
    inv_final = lax.rsqrt(mean_row(output * output) + epsilon)
    wanted = weighted[...]
    grad_out = inv_final * wanted - output * (inv_final * inv_final * inv_final) * mean_row(
        wanted * output
    )
    grad_output[...] = grad_out
    post_grad = post_gain[...] * grad_out
    grad_mlp[...] = inv_post * post_grad - mlp_out * (inv_post * inv_post * inv_post) * mean_row(
        post_grad * mlp_out
    )
    value = grad_mlp[:, mine].astype(BF16)
    for peer in range(out.shape[0]):
        out[peer] = value


def backward_kernel(core, own, other, gate, up, w_gate, w_up, w_down, send, grad_gate, grad_up):
    mine, theirs = halves(core, own.shape[1])
    grad_hidden = dot_nt(own[...], w_down[:, mine]) + dot_nt(other[...], w_down[:, theirs])
    gate_pre = gate[...]
    to_gate = (grad_hidden * up[...] * gelu_slope(gate_pre)).astype(BF16)
    to_up = (grad_hidden * gelu_tanh(gate_pre)).astype(BF16)
    grad_gate[...] = to_gate
    grad_up[...] = to_up
    send[...] = (dot_nn(to_gate, w_gate[:, theirs]) + dot_nn(to_up, w_up[:, theirs])).astype(BF16)


def backward_sum_kernel(core, grad_gate, grad_up, w_gate, w_up, arrived, out):
    mine, _ = halves(core, arrived.shape[1])
    total = dot_nn(grad_gate[...], w_gate[:, mine]) + dot_nn(grad_up[...], w_up[:, mine])
    out[...] = (total + arrived[...].astype(F32)).astype(BF16).reshape(out.shape)


def input_kernel(core, pieces, stream, grad_output, pre_gain, out, grad_stream):
    mine, _ = halves(core, out.shape[2])
    rows = stream[...].astype(F32)
    inv_pre = lax.rsqrt(mean_row(rows * rows) + epsilon)
    pre_grad = pre_gain[...] * column_total(pieces)
    grad_stream[...] = (
        grad_output[...]
        + inv_pre * pre_grad
        - rows * (inv_pre * inv_pre * inv_pre) * mean_row(pre_grad * rows)
    )
    value = grad_stream[:, mine].astype(BF16)
    for peer in range(out.shape[0]):
        out[peer] = value


def change_kernel(core, own, other, own_corrupt, other_corrupt, w_enc, b_enc, out):
    width = own.shape[1]
    first, second = halves(core, width)
    bias = b_enc[...]

    def code(a, b):
        return jax.nn.relu(dot_nn(a[...], w_enc[first, :]) + dot_nn(b[...], w_enc[second, :]) + bias)

    out[...] = code(own, other) - code(own_corrupt, other_corrupt)


def attribution_kernel(core, own, other, w_dec, change, out):
    mine, theirs = halves(core, own.shape[1])
    projected = dot_nt(own[...], w_dec[:, mine]) + dot_nt(other[...], w_dec[:, theirs])
    out[...] = jnp.sum(change[...] * projected, axis=0, keepdims=True)


def exchanged(blocks, axes):
    return lax.all_to_all(blocks, axes, 0, 0, tiled=True)


def swapped(value):
    return lax.ppermute(value, "core", SWAP)


def local(
    resid_clean,
    resid_corrupt,
    answer_ids,
    unembed,
    pre_gain,
    post_gain,
    final_gain,
    w_gate,
    w_up,
    w_down,
    w_enc,
    b_enc,
    w_dec,
):
    width = resid_clean.shape[1]
    half = width // 2
    column, plane = lax.axis_size(COLUMN), lax.axis_size(PLANE)
    tokens = column * plane
    core_index = lax.axis_index("core")
    core = core_index.astype(jnp.int32).reshape(1)
    hidden_units, latents = w_gate.shape[1], w_enc.shape[1]
    w_gate, w_up = w_gate.T, w_up.T
    pre_gain, post_gain, final_gain = (g[None] for g in (pre_gain, post_gain, final_gain))

    both = jnp.concatenate([resid_clean, resid_corrupt], axis=0)
    mixed = exchanged(jnp.broadcast_to(both[None], (column, 2, width)), COLUMN)
    stream = mixed[:, 0]
    corrupt = mixed[:, 1]

    def spread(block):
        mine = lax.dynamic_slice_in_dim(block, core_index * half, half, 1)
        return jnp.broadcast_to(mine[None], (plane, column, half))

    def gathered(blocks):
        own = exchanged(blocks, PLANE).reshape(tokens, half)
        return own, swapped(own)

    blocks = shape((plane, column, half), BF16)
    peers = shape((column, column, half), BF16)
    rows = shape((column, width), F32)
    send = shape((tokens, half), BF16)
    units = shape((tokens, hidden_units), BF16)
    units32 = shape((tokens, hidden_units), F32)

    own, other = gathered(spread(stream))
    sent, hidden, gate, up = call(
        forward_kernel,
        (send, units, units32, units32),
        core, own, other, w_gate, w_up, w_down, pre_gain,
        scratch=[pltpu.VMEM((tokens, width), BF16)],
    )
    pieces = call(forward_sum_kernel, blocks, core, hidden, w_down, swapped(sent))
    pieces = call(plane_sum_kernel, peers, exchanged(pieces, PLANE))

    place = lax.axis_index(PLANE)
    answers = lax.dynamic_slice_in_dim(answer_ids.reshape(column, plane, 2), place, 1, 1)[:, 0]
    weighted = call(direction_kernel, rows, answers, unembed, final_gain)
    spread_grad, grad_output = call(
        output_kernel,
        (blocks, rows),
        core, exchanged(pieces, COLUMN), stream, weighted, post_gain,
        scratch=[pltpu.VMEM((column, width), F32)],
    )

    grad_own, grad_other = gathered(spread_grad)
    sent, grad_gate, grad_up = call(
        backward_kernel,
        (send, units, units),
        core, grad_own, grad_other, gate, up, w_gate, w_up, w_down,
    )
    pieces = call(
        backward_sum_kernel, blocks, core, grad_gate, grad_up, w_gate, w_up, swapped(sent)
    )
    pieces = call(plane_sum_kernel, peers, exchanged(pieces, PLANE))
    spread_stream = call(
        input_kernel,
        blocks,
        core, exchanged(pieces, COLUMN), stream, grad_output, pre_gain,
        scratch=[pltpu.VMEM((column, width), F32)],
    )

    own_corrupt, other_corrupt = gathered(spread(corrupt))
    change = call(
        change_kernel,
        shape((tokens, latents), F32),
        core, own, other, own_corrupt, other_corrupt, w_enc, b_enc[None],
    )
    last_own, last_other = gathered(spread_stream)
    return call(
        attribution_kernel, shape((1, latents), F32), core, last_own, last_other, w_dec, change
    )


def solution(mesh):
    fine = Mesh(mesh.devices.reshape(2, 2, 2, 4, 4), DEVICES)
    return jax.shard_map(
        local,
        mesh=fine,
        in_specs=(
            P(DEVICES, None),
            P(DEVICES, None),
            P(),
            P(),
            P(),
            P(),
            P(),
            P(None, DEVICES),
            P(None, DEVICES),
            P(DEVICES, None),
            P(None, DEVICES),
            P(DEVICES),
            P(DEVICES, None),
        ),
        out_specs=P(None, DEVICES),
        check_vma=False,
    )
```

```python
import jax
import jax.numpy as jnp
from jax import lax
from jax.experimental import pallas as pl
from jax.experimental.pallas import tpu as pltpu
from jax.sharding import Mesh
from jax.sharding import PartitionSpec as P

epsilon = 1e-06
gelu_scale = 0.7978845608028654
gelu_cubic = 0.044715

DEVICES = ("y_lo", "core", "y_hi", "x", "z")
CHIPS = ("x", "z", "y_lo", "y_hi")
SWAP = [(0, 1), (1, 0)]
F32 = jnp.float32
BF16 = jnp.bfloat16
VMEM = pl.BlockSpec(memory_space=pltpu.VMEM)
SMEM = pl.BlockSpec(memory_space=pltpu.SMEM)


def shape(dims, dtype):
    return jax.ShapeDtypeStruct(dims, dtype)


def call(kernel, outs, *args, space=pltpu.VMEM, scratch=()):
    return pl.pallas_call(
        kernel,
        out_shape=jax.tree.map(lambda o: space(o.shape, o.dtype), outs),
        in_specs=[SMEM if a.dtype == jnp.int32 else VMEM for a in args],
        out_specs=jax.tree.map(lambda _: VMEM, outs),
        scratch_shapes=scratch,
        compiler_params=pltpu.CompilerParams(vmem_limit_bytes=8 << 20),
    )(
        *(
            a if a.dtype == jnp.int32 else pltpu.with_memory_space_constraint(a, pltpu.VMEM)
            for a in args
        )
    )


def gelu_tanh(value):
    return 0.5 * value * (1.0 + jnp.tanh(gelu_scale * (value + gelu_cubic * value * value * value)))


def gelu_slope(value):
    inner = jnp.tanh(gelu_scale * (value + gelu_cubic * value * value * value))
    return 0.5 * (1.0 + inner) + 0.5 * value * (1.0 - inner * inner) * gelu_scale * (
        1.0 + 3.0 * gelu_cubic * value * value
    )


def dot_nn(left, right):
    return jnp.dot(left, right, preferred_element_type=F32)


def dot_nt(left, right):
    return lax.dot_general(left, right, (((1,), (1,)), ((), ())), preferred_element_type=F32)


def mean_row(value):
    return jnp.mean(value, axis=-1, keepdims=True)


def halves(core_ref, width):
    core = core_ref[0]
    return (
        pl.ds(pl.multiple_of(core * width, 128), width),
        pl.ds(pl.multiple_of((1 - core) * width, 128), width),
    )


def merge_kernel(clean, corrupt, out):
    out[0:1] = clean[...]
    out[1:2] = corrupt[...]


def spread(value, out):
    for chip in range(out.shape[0]):
        out[chip] = value


def chip_rows_kernel(where, both, partner, out, stream):
    first = where[0] == 0
    mine, _ = halves(where, out.shape[2])
    a, b = both[...].astype(F32), partner[...].astype(F32)
    low, high = jnp.where(first, a, b), jnp.where(first, b, a)
    stream[0:1] = low[0:1]
    stream[1:2] = high[0:1]
    a, b = both[:, mine].astype(F32), partner[:, mine].astype(F32)
    low, high = jnp.where(first, a, b), jnp.where(first, b, a)
    quad = jnp.concatenate([low[0:1], high[0:1], low[1:2], high[1:2]], axis=0)
    spread(quad.astype(BF16), out)


def rows_kernel(pieces, clean, corrupt):
    clean[...] = pieces[:, :2].reshape(clean.shape)
    corrupt[...] = pieces[:, 2:].reshape(corrupt.shape)


def forward_kernel(where, own, other, w_gate, w_up, w_down, gain, send, hidden, gate, up, normed):
    width = own.shape[1]
    mine, theirs = halves(where, width)
    a, b = own[...].astype(F32), other[...].astype(F32)
    total = jnp.sum(a * a, axis=-1, keepdims=True) + jnp.sum(b * b, axis=-1, keepdims=True)
    inv = lax.rsqrt(total / (2 * width) + epsilon)
    normed[:, mine] = (a * inv * gain[:, mine]).astype(BF16)
    normed[:, theirs] = (b * inv * gain[:, theirs]).astype(BF16)
    gate_pre = dot_nt(normed[...], w_gate[...])
    up_proj = dot_nt(normed[...], w_up[...])
    gate[...] = gate_pre
    up[...] = up_proj
    act = (gelu_tanh(gate_pre) * up_proj).astype(BF16)
    hidden[...] = act
    send[...] = dot_nn(act, w_down[:, theirs]).astype(BF16)


def forward_own_kernel(where, hidden, w_down, out):
    mine, _ = halves(where, out.shape[1])
    out[...] = dot_nn(hidden[...], w_down[:, mine])


def chip_sum_kernel(own, arrived, out):
    out[...] = (own[...] + arrived[...].astype(F32)).astype(BF16).reshape(out.shape)


def total_kernel(pieces, out):
    rows = pieces.shape[0] * pieces.shape[1]
    token = lax.broadcasted_iota(jnp.int32, (8, rows), 0)
    source = lax.broadcasted_iota(jnp.int32, (8, rows), 1)
    pick = (source % 2 == token).astype(F32).astype(BF16)
    out[...] = dot_nn(pick, pieces[...].reshape(rows, out.shape[1]))[: out.shape[0]]


def joined(where, own, other, out):
    mine, theirs = halves(where, own.shape[1])
    out[:, mine] = own[...]
    out[:, theirs] = other[...]
    return out[...]


def wanted_rows(where, answers, unembed, gain):
    lanes = lax.broadcasted_iota(jnp.int32, (1, unembed.shape[0]), 1)
    rows = []
    for core in range(2):
        token = where[1 + core]
        rows.append(
            (lanes == answers[0, token]).astype(F32) - (lanes == answers[1, token]).astype(F32)
        )
    selector = jnp.concatenate(rows + rows + rows + rows, axis=0).astype(BF16)
    return gain[...] * dot_nn(selector, unembed[...])[:2]


def output_kernel(
    where,
    answers,
    own,
    other,
    stream,
    unembed,
    final_gain,
    post_gain,
    out,
    grad_output,
    whole,
):
    mine, _ = halves(where, out.shape[2])
    mlp_out = joined(where, own, other, whole)
    inv_post = lax.rsqrt(mean_row(mlp_out * mlp_out) + epsilon)
    output = stream[...] + mlp_out * inv_post * post_gain[...]
    inv_final = lax.rsqrt(mean_row(output * output) + epsilon)
    wanted = wanted_rows(where, answers, unembed, final_gain)
    grad_out = inv_final * wanted - output * (inv_final * inv_final * inv_final) * mean_row(
        wanted * output
    )
    grad_output[...] = grad_out
    post_grad = post_gain[...] * grad_out
    whole[...] = inv_post * post_grad - mlp_out * (inv_post * inv_post * inv_post) * mean_row(
        post_grad * mlp_out
    )
    spread(whole[:, mine].astype(BF16), out)


def backward_own_half_kernel(where, own, w_down, out):
    mine, _ = halves(where, own.shape[2])
    out[...] = dot_nt(own[...].reshape(out.shape[0], own.shape[2]), w_down[:, mine])


def backward_kernel(
    where, own_part, other, gate, up, w_gate, w_up, w_down, send, grad_gate, grad_up
):
    width = other.shape[2]
    _, theirs = halves(where, width)
    grad_hidden = own_part[...] + dot_nt(
        other[...].reshape(own_part.shape[0], width), w_down[:, theirs]
    )
    gate_pre = gate[...]
    to_gate = (grad_hidden * up[...] * gelu_slope(gate_pre)).astype(BF16)
    to_up = (grad_hidden * gelu_tanh(gate_pre)).astype(BF16)
    grad_gate[...] = to_gate
    grad_up[...] = to_up
    send[...] = (dot_nn(to_gate, w_gate[:, theirs]) + dot_nn(to_up, w_up[:, theirs])).astype(BF16)


def backward_own_kernel(where, grad_gate, grad_up, w_gate, w_up, out):
    mine, _ = halves(where, out.shape[1])
    out[...] = dot_nn(grad_gate[...], w_gate[:, mine]) + dot_nn(grad_up[...], w_up[:, mine])


def input_kernel(where, own, other, stream, grad_output, pre_gain, out, whole):
    mine, _ = halves(where, out.shape[2])
    rows = stream[...]
    inv_pre = lax.rsqrt(mean_row(rows * rows) + epsilon)
    pre_grad = pre_gain[...] * joined(where, own, other, whole)
    whole[...] = (
        grad_output[...]
        + inv_pre * pre_grad
        - rows * (inv_pre * inv_pre * inv_pre) * mean_row(pre_grad * rows)
    )
    spread(whole[:, mine].astype(BF16), out)


def code_of(where, own, other, w_enc, b_enc):
    first, second = halves(where, own.shape[1])
    return jax.nn.relu(
        dot_nn(own[...], w_enc[first, :]) + dot_nn(other[...], w_enc[second, :]) + b_enc[...]
    )


def code_kernel(where, own, other, w_enc, b_enc, out):
    out[...] = code_of(where, own, other, w_enc, b_enc)


def change_kernel(where, own, other, w_enc, b_enc, clean_code, out):
    out[...] = clean_code[...] - code_of(where, own, other, w_enc, b_enc)


def attribution_own_kernel(where, own, w_dec, out):
    mine, _ = halves(where, own.shape[2])
    out[...] = dot_nt(own[...].reshape(out.shape[0], own.shape[2]), w_dec[:, mine])


def attribution_kernel(where, part, other, w_dec, change, out):
    width = other.shape[2]
    _, theirs = halves(where, width)
    projected = part[...] + dot_nt(other[...].reshape(part.shape[0], width), w_dec[:, theirs])
    out[...] = jnp.sum(change[...] * projected, axis=0, keepdims=True)


def exchanged(blocks):
    return lax.all_to_all(blocks, CHIPS, 0, 0, tiled=True)


def swapped(value):
    return lax.ppermute(value, "core", SWAP)


def local(
    resid_clean,
    resid_corrupt,
    answer_ids,
    unembed,
    pre_gain,
    post_gain,
    final_gain,
    w_gate,
    w_up,
    w_down,
    w_enc,
    b_enc,
    w_dec,
):
    width = resid_clean.shape[1]
    half = width // 2
    chips, plane = lax.axis_size(CHIPS), lax.axis_size(("x", "z"))
    tokens = 2 * chips
    core_index = lax.axis_index("core")
    pair = (
        lax.axis_index("y_lo") * (4 * plane)
        + lax.axis_index("y_hi") * plane
        + lax.axis_index(("x", "z"))
    )
    where = jnp.stack([core_index, pair, pair + 2 * plane]).astype(jnp.int32)
    hidden_units, latents = w_gate.shape[1], w_enc.shape[1]
    w_gate, w_up = w_gate.T, w_up.T
    gains = (g[None] for g in (pre_gain, post_gain, final_gain))
    b_enc = b_enc[None]

    halved = shape((tokens, half), BF16)
    halved32 = shape((tokens, half), F32)
    pairs = shape((chips, 2, half), BF16)
    pair_rows = shape((2, width), F32)
    pair_half = shape((2, half), F32)
    units = shape((tokens, hidden_units), BF16)
    units32 = shape((tokens, hidden_units), F32)
    codes = shape((tokens, latents), F32)
    whole = pltpu.VMEM((2, width), F32)

    both = call(merge_kernel, shape((2, width), BF16), resid_clean, resid_corrupt)
    partner = swapped(both)
    partner, where, pre_gain, post_gain, final_gain = lax.optimization_barrier(
        (partner, where, *gains)
    )
    quads, stream = call(
        chip_rows_kernel, (shape((chips, 4, half), BF16), pair_rows), where, both, partner
    )
    own, own_corrupt = call(rows_kernel, (halved, halved), exchanged(quads))
    other = swapped(own)
    other, own_corrupt = lax.optimization_barrier((other, own_corrupt))
    other_corrupt = swapped(own_corrupt)

    sent, hidden, gate, up = call(
        forward_kernel,
        (halved, units, units32, units32),
        where, own, other, w_gate, w_up, w_down, pre_gain,
        scratch=[pltpu.VMEM((tokens, width), BF16)],
    )
    sent, other_corrupt = lax.optimization_barrier((sent, other_corrupt))
    arrived = swapped(sent)
    own_sum = call(forward_own_kernel, halved32, where, hidden, w_down)
    own_sum, own, other = lax.optimization_barrier((own_sum, own, other))
    clean_code = call(code_kernel, codes, where, own, other, w_enc, b_enc)
    arrived, own_sum, clean_code = lax.optimization_barrier((arrived, own_sum, clean_code))
    own_mlp = call(
        total_kernel, pair_half, exchanged(call(chip_sum_kernel, pairs, own_sum, arrived))
    )
    own_mlp, own_corrupt = lax.optimization_barrier((own_mlp, own_corrupt))
    other_mlp = swapped(own_mlp)
    change = call(
        change_kernel, codes, where, own_corrupt, other_corrupt, w_enc, b_enc, clean_code
    )
    other_mlp, change = lax.optimization_barrier((other_mlp, change))
    spread_grad, grad_output = call(
        output_kernel,
        (pairs, pair_rows),
        where, answer_ids.T, own_mlp, other_mlp, stream, unembed, final_gain, post_gain,
        scratch=[whole],
    )

    grad_own = exchanged(spread_grad)
    grad_other = swapped(grad_own)
    own_part = call(backward_own_half_kernel, units32, where, grad_own, w_down)
    grad_other, own_part = lax.optimization_barrier((grad_other, own_part))
    sent, grad_gate, grad_up = call(
        backward_kernel,
        (halved, units, units),
        where, own_part, grad_other, gate, up, w_gate, w_up, w_down,
    )
    arrived = swapped(sent)
    own_sum = call(backward_own_kernel, halved32, where, grad_gate, grad_up, w_gate, w_up)
    arrived, own_sum = lax.optimization_barrier((arrived, own_sum))
    own_normed = call(
        total_kernel, pair_half, exchanged(call(chip_sum_kernel, pairs, own_sum, arrived))
    )
    spread_stream = call(
        input_kernel,
        pairs,
        where, own_normed, swapped(own_normed), stream, grad_output, pre_gain,
        scratch=[whole],
    )

    last_own = exchanged(spread_stream)
    last_other = swapped(last_own)
    own_part = call(attribution_own_kernel, codes, where, last_own, w_dec)
    last_other, own_part = lax.optimization_barrier((last_other, own_part))
    return call(
        attribution_kernel,
        shape((1, latents), F32),
        where, own_part, last_other, w_dec, change,
        space=jax.ShapeDtypeStruct,
    )


def solution(mesh):
    fine = Mesh(mesh.devices.reshape(2, 2, 2, 4, 4), DEVICES)
    return jax.shard_map(
        local,
        mesh=fine,
        in_specs=(
            P(DEVICES, None),
            P(DEVICES, None),
            P(),
            P(),
            P(),
            P(),
            P(),
            P(None, DEVICES),
            P(None, DEVICES),
            P(DEVICES, None),
            P(None, DEVICES),
            P(DEVICES),
            P(DEVICES, None),
        ),
        out_specs=P(None, DEVICES),
        check_vma=False,
    )
```

```python
import jax
import jax.numpy as jnp
from jax import lax
from jax.experimental import pallas as pl
from jax.experimental.pallas import tpu as pltpu
from jax.sharding import Mesh
from jax.sharding import PartitionSpec as P

epsilon = 1e-06
gelu_scale = 0.7978845608028654
gelu_cubic = 0.044715

DEVICES = ("y_lo", "core", "y_hi", "x", "z")
CHIPS = ("x", "z", "y_lo", "y_hi")
SWAP = [(0, 1), (1, 0)]
LIMIT = 16 << 20
HINT = 10**10
F32 = jnp.float32
BF16 = jnp.bfloat16
VMEM = pl.BlockSpec(memory_space=pltpu.VMEM)
SMEM = pl.BlockSpec(memory_space=pltpu.SMEM)


def shape(dims, dtype):
    return jax.ShapeDtypeStruct(dims, dtype)


def call(kernel, outs, *args, space=pltpu.VMEM, scratch=(), flops=0, source=pltpu.VMEM):
    return pl.pallas_call(
        kernel,
        out_shape=jax.tree.map(lambda o: space(o.shape, o.dtype), outs),
        in_specs=[
            SMEM if a.dtype == jnp.int32 else pl.BlockSpec(memory_space=source) for a in args
        ],
        out_specs=jax.tree.map(lambda _: VMEM, outs),
        scratch_shapes=scratch,
        compiler_params=pltpu.CompilerParams(vmem_limit_bytes=LIMIT),
        cost_estimate=pl.CostEstimate(flops=flops, transcendentals=0, bytes_accessed=0)
        if flops
        else None,
    )(
        *(
            a if a.dtype == jnp.int32 else pltpu.with_memory_space_constraint(a, source)
            for a in args
        )
    )


def gelu_tanh(value):
    return 0.5 * value * (1.0 + jnp.tanh(gelu_scale * (value + gelu_cubic * value * value * value)))


def gelu_slope(value):
    inner = jnp.tanh(gelu_scale * (value + gelu_cubic * value * value * value))
    return 0.5 * (1.0 + inner) + 0.5 * value * (1.0 - inner * inner) * gelu_scale * (
        1.0 + 3.0 * gelu_cubic * value * value
    )


def dot_nn(left, right):
    return jnp.dot(left, right, preferred_element_type=F32)


def dot_nt(left, right):
    return lax.dot_general(left, right, (((1,), (1,)), ((), ())), preferred_element_type=F32)


def mean_row(value):
    return jnp.mean(value, axis=-1, keepdims=True)


def halves(core_ref, width):
    core = core_ref[0]
    return (
        pl.ds(pl.multiple_of(core * width, 128), width),
        pl.ds(pl.multiple_of((1 - core) * width, 128), width),
    )


def spread(value, out):
    for chip in range(out.shape[0]):
        out[chip] = value


def load_kernel(clean, corrupt, own_clean, own_corrupt, sems):
    copies = [
        pltpu.make_async_copy(clean, own_clean, sems.at[0]),
        pltpu.make_async_copy(corrupt, own_corrupt, sems.at[1]),
    ]
    for copy in copies:
        copy.start()
    for copy in copies:
        copy.wait()


def gains_kernel(pre, post, final, out):
    for i, gain in enumerate((pre, post, final)):
        out[i : i + 1] = gain[...].reshape(1, gain.shape[0])


def chip_rows_kernel(where, clean, corrupt, other_clean, other_corrupt, out, stream, rows):
    first = where[0] == 0
    mine, _ = halves(where, out.shape[2])
    for i, (a, b) in enumerate(((clean, other_clean), (corrupt, other_corrupt))):
        a, b = a[...].astype(F32), b[...].astype(F32)
        rows[2 * i : 2 * i + 1] = jnp.where(first, a, b)
        rows[2 * i + 1 : 2 * i + 2] = jnp.where(first, b, a)
    stream[...] = rows[0:2]
    spread(rows[:, mine].astype(BF16), out)


def rows_kernel(pieces, clean, corrupt):
    clean[...] = pieces[:, :2].reshape(clean.shape)
    corrupt[...] = pieces[:, 2:].reshape(corrupt.shape)


def forward_kernel(where, own, other, w_gate, w_up, w_down, gain, send, hidden, gate, up, normed):
    width = own.shape[1]
    mine, theirs = halves(where, width)
    a, b = own[...].astype(F32), other[...].astype(F32)
    total = jnp.sum(a * a, axis=-1, keepdims=True) + jnp.sum(b * b, axis=-1, keepdims=True)
    inv = lax.rsqrt(total / (2 * width) + epsilon)
    normed[:, mine] = (a * inv * gain[0:1, mine]).astype(BF16)
    normed[:, theirs] = (b * inv * gain[0:1, theirs]).astype(BF16)
    gate_pre = dot_nt(normed[...], w_gate[...])
    up_proj = dot_nt(normed[...], w_up[...])
    gate[...] = gate_pre
    up[...] = up_proj
    act = (gelu_tanh(gate_pre) * up_proj).astype(BF16)
    hidden[...] = act
    send[...] = dot_nn(act, w_down[:, theirs]).astype(BF16)


def forward_own_kernel(where, hidden, w_down, out):
    mine, _ = halves(where, out.shape[1])
    out[...] = dot_nn(hidden[...], w_down[:, mine])


def chip_sum_kernel(own, arrived, out):
    out[...] = (own[...] + arrived[...].astype(F32)).astype(BF16).reshape(out.shape)


def total_kernel(pieces, out):
    rows = pieces.shape[0] * pieces.shape[1]
    token = lax.broadcasted_iota(jnp.int32, (8, rows), 0)
    source = lax.broadcasted_iota(jnp.int32, (8, rows), 1)
    pick = (source % 2 == token).astype(F32).astype(BF16)
    out[...] = dot_nn(pick, pieces[...].reshape(rows, out.shape[1]))[: out.shape[0]]


def joined(where, own, other, out):
    mine, theirs = halves(where, own.shape[1])
    out[:, mine] = own[...]
    out[:, theirs] = other[...]
    return out[...]


def wanted_kernel(where, answers, unembed, gains, out):
    lanes = lax.broadcasted_iota(jnp.int32, (1, unembed.shape[0]), 1)
    rows = []
    for core in range(2):
        token = where[1 + core]
        rows.append(
            (lanes == answers[0, token]).astype(F32) - (lanes == answers[1, token]).astype(F32)
        )
    selector = jnp.concatenate(rows * 4, axis=0).astype(BF16)
    out[...] = gains[2:3] * dot_nn(selector, unembed[...])[:2]


def output_kernel(
    where, own, other, stream, weighted, gains, out, grad_output, whole
):
    mine, _ = halves(where, out.shape[2])
    post_gain = gains[1:2]
    mlp_out = joined(where, own, other, whole)
    inv_post = lax.rsqrt(mean_row(mlp_out * mlp_out) + epsilon)
    output = stream[...] + mlp_out * inv_post * post_gain
    inv_final = lax.rsqrt(mean_row(output * output) + epsilon)
    wanted = weighted[...]
    grad_out = inv_final * wanted - output * (inv_final * inv_final * inv_final) * mean_row(
        wanted * output
    )
    grad_output[...] = grad_out
    post_grad = post_gain * grad_out
    whole[...] = inv_post * post_grad - mlp_out * (inv_post * inv_post * inv_post) * mean_row(
        post_grad * mlp_out
    )
    spread(whole[:, mine].astype(BF16), out)


def backward_own_half_kernel(where, own, w_down, out):
    mine, _ = halves(where, own.shape[2])
    out[...] = dot_nt(own[...].reshape(out.shape[0], own.shape[2]), w_down[:, mine])


def backward_kernel(
    where, own_part, other, gate, up, w_gate, w_up, w_down, send, grad_gate, grad_up
):
    width = other.shape[2]
    _, theirs = halves(where, width)
    grad_hidden = own_part[...] + dot_nt(
        other[...].reshape(own_part.shape[0], width), w_down[:, theirs]
    )
    gate_pre = gate[...]
    to_gate = (grad_hidden * up[...] * gelu_slope(gate_pre)).astype(BF16)
    to_up = (grad_hidden * gelu_tanh(gate_pre)).astype(BF16)
    grad_gate[...] = to_gate
    grad_up[...] = to_up
    send[...] = (dot_nn(to_gate, w_gate[:, theirs]) + dot_nn(to_up, w_up[:, theirs])).astype(BF16)


def backward_own_kernel(where, grad_gate, grad_up, w_gate, w_up, out):
    mine, _ = halves(where, out.shape[1])
    out[...] = dot_nn(grad_gate[...], w_gate[:, mine]) + dot_nn(grad_up[...], w_up[:, mine])


def input_kernel(where, own, other, stream, grad_output, gains, out, whole):
    mine, _ = halves(where, out.shape[2])
    rows = stream[...]
    inv_pre = lax.rsqrt(mean_row(rows * rows) + epsilon)
    pre_grad = gains[0:1] * joined(where, own, other, whole)
    whole[...] = (
        grad_output[...]
        + inv_pre * pre_grad
        - rows * (inv_pre * inv_pre * inv_pre) * mean_row(pre_grad * rows)
    )
    spread(whole[:, mine].astype(BF16), out)


def code_of(where, own, other, w_enc, b_enc):
    first, second = halves(where, own.shape[1])
    return jax.nn.relu(
        dot_nn(own[...], w_enc[first, :]) + dot_nn(other[...], w_enc[second, :]) + b_enc[...]
    )


def code_kernel(where, own, other, w_enc, b_enc, out):
    out[...] = code_of(where, own, other, w_enc, b_enc)


def change_kernel(where, own, other, w_enc, b_enc, clean_code, out):
    out[...] = clean_code[...] - code_of(where, own, other, w_enc, b_enc)


def attribution_own_kernel(where, own, w_dec, out):
    mine, _ = halves(where, own.shape[2])
    out[...] = dot_nt(own[...].reshape(out.shape[0], own.shape[2]), w_dec[:, mine])


def attribution_kernel(where, part, other, w_dec, change, out):
    width = other.shape[2]
    _, theirs = halves(where, width)
    projected = part[...] + dot_nt(other[...].reshape(part.shape[0], width), w_dec[:, theirs])
    out[...] = jnp.sum(change[...] * projected, axis=0, keepdims=True)


def exchanged(blocks):
    return lax.all_to_all(blocks, CHIPS, 0, 0, tiled=True)


def swapped(value):
    return lax.ppermute(value, "core", SWAP)


def local(
    resid_clean,
    resid_corrupt,
    answer_ids,
    unembed,
    pre_gain,
    post_gain,
    final_gain,
    w_gate,
    w_up,
    w_down,
    w_enc,
    b_enc,
    w_dec,
):
    width = resid_clean.shape[1]
    half = width // 2
    chips, plane = lax.axis_size(CHIPS), lax.axis_size(("x", "z"))
    tokens = 2 * chips
    core_index = lax.axis_index("core")
    pair = (
        lax.axis_index("y_lo") * (4 * plane)
        + lax.axis_index("y_hi") * plane
        + lax.axis_index(("x", "z"))
    )
    where = jnp.stack([core_index, pair, pair + 2 * plane]).astype(jnp.int32)
    hidden_units, latents = w_gate.shape[1], w_enc.shape[1]
    w_gate, w_up = w_gate.T, w_up.T
    b_enc = b_enc[None]

    halved = shape((tokens, half), BF16)
    halved32 = shape((tokens, half), F32)
    pairs = shape((chips, 2, half), BF16)
    pair_rows = shape((2, width), F32)
    pair_half = shape((2, half), F32)
    units = shape((tokens, hidden_units), BF16)
    units32 = shape((tokens, hidden_units), F32)
    codes = shape((tokens, latents), F32)
    whole = pltpu.VMEM((2, width), F32)

    partner = (swapped(resid_clean), swapped(resid_corrupt))
    one_row = shape((1, width), BF16)
    held = call(
        load_kernel,
        (one_row, one_row),
        resid_clean, resid_corrupt,
        source=pltpu.HBM,
        scratch=[pltpu.SemaphoreType.DMA((2,))],
    )
    *partner, where, clean, corrupt = lax.optimization_barrier((*partner, where, *held))
    quads, stream = call(
        chip_rows_kernel,
        (shape((chips, 4, half), BF16), pair_rows),
        where, clean, corrupt, *partner,
        scratch=[pltpu.VMEM((4, width), F32)],
        flops=HINT,
    )
    own, own_corrupt = call(rows_kernel, (halved, halved), exchanged(quads), flops=HINT)
    pre_gain, own_corrupt = lax.optimization_barrier((pre_gain, own_corrupt))
    gains = call(gains_kernel, shape((3, width), F32), pre_gain, post_gain, final_gain)
    weighted = call(wanted_kernel, pair_rows, where, answer_ids.T, unembed, gains)
    other = swapped(own)
    other, own_corrupt, gains, weighted = lax.optimization_barrier(
        (other, own_corrupt, gains, weighted)
    )
    other_corrupt = swapped(own_corrupt)

    sent, hidden, gate, up = call(
        forward_kernel,
        (halved, units, units32, units32),
        where, own, other, w_gate, w_up, w_down, gains,
        scratch=[pltpu.VMEM((tokens, width), BF16)],
    )
    sent, other_corrupt = lax.optimization_barrier((sent, other_corrupt))
    arrived = swapped(sent)
    own_sum = call(forward_own_kernel, halved32, where, hidden, w_down)
    own_sum, own, other = lax.optimization_barrier((own_sum, own, other))
    clean_code = call(code_kernel, codes, where, own, other, w_enc, b_enc)
    arrived, own_sum, clean_code = lax.optimization_barrier((arrived, own_sum, clean_code))
    own_mlp = call(
        total_kernel, pair_half, exchanged(call(chip_sum_kernel, pairs, own_sum, arrived))
    )
    own_mlp, own_corrupt = lax.optimization_barrier((own_mlp, own_corrupt))
    other_mlp = swapped(own_mlp)
    change = call(
        change_kernel, codes, where, own_corrupt, other_corrupt, w_enc, b_enc, clean_code
    )
    other_mlp, change = lax.optimization_barrier((other_mlp, change))
    spread_grad, grad_output = call(
        output_kernel,
        (pairs, pair_rows),
        where, own_mlp, other_mlp, stream, weighted, gains,
        scratch=[whole],
    )

    grad_own = exchanged(spread_grad)
    grad_other = swapped(grad_own)
    own_part = call(backward_own_half_kernel, units32, where, grad_own, w_down)
    grad_other, own_part = lax.optimization_barrier((grad_other, own_part))
    sent, grad_gate, grad_up = call(
        backward_kernel,
        (halved, units, units),
        where, own_part, grad_other, gate, up, w_gate, w_up, w_down,
    )
    arrived = swapped(sent)
    own_sum = call(backward_own_kernel, halved32, where, grad_gate, grad_up, w_gate, w_up)
    arrived, own_sum = lax.optimization_barrier((arrived, own_sum))
    own_normed = call(
        total_kernel, pair_half, exchanged(call(chip_sum_kernel, pairs, own_sum, arrived))
    )
    spread_stream = call(
        input_kernel,
        pairs,
        where, own_normed, swapped(own_normed), stream, grad_output, gains,
        scratch=[whole],
    )

    last_own = exchanged(spread_stream)
    last_other = swapped(last_own)
    own_part = call(attribution_own_kernel, codes, where, last_own, w_dec)
    last_other, own_part = lax.optimization_barrier((last_other, own_part))
    return call(
        attribution_kernel,
        shape((1, latents), F32),
        where, own_part, last_other, w_dec, change,
        space=jax.ShapeDtypeStruct,
    )


def solution(mesh):
    fine = Mesh(mesh.devices.reshape(2, 2, 2, 4, 4), DEVICES)
    return jax.shard_map(
        local,
        mesh=fine,
        in_specs=(
            P(DEVICES, None),
            P(DEVICES, None),
            P(),
            P(),
            P(),
            P(),
            P(),
            P(None, DEVICES),
            P(None, DEVICES),
            P(DEVICES, None),
            P(None, DEVICES),
            P(DEVICES),
            P(DEVICES, None),
        ),
        out_specs=P(None, DEVICES),
        check_vma=False,
    )
```

```python
import jax
import jax.numpy as jnp
from jax import lax
from jax.experimental import pallas as pl
from jax.experimental.pallas import tpu as pltpu
from jax.sharding import Mesh
from jax.sharding import PartitionSpec as P

epsilon = 1e-06
gelu_scale = 0.7978845608028654
gelu_cubic = 0.044715

DEVICES = ("y_lo", "core", "y_hi", "x", "z")
CHIPS = ("x", "z", "y_lo", "y_hi")
SWAP = [(0, 1), (1, 0)]
LIMIT = 16 << 20
HINT = 10**11
CHUNK = 768
F32 = jnp.float32
BF16 = jnp.bfloat16
VMEM = pl.BlockSpec(memory_space=pltpu.VMEM)
SMEM = pl.BlockSpec(memory_space=pltpu.SMEM)


def shape(dims, dtype):
    return jax.ShapeDtypeStruct(dims, dtype)


def call(kernel, outs, *args, space=pltpu.VMEM, scratch=(), flops=0, source=pltpu.VMEM):
    return pl.pallas_call(
        kernel,
        out_shape=jax.tree.map(lambda o: space(o.shape, o.dtype), outs),
        in_specs=[
            SMEM if a.dtype == jnp.int32 else pl.BlockSpec(memory_space=source) for a in args
        ],
        out_specs=jax.tree.map(lambda _: VMEM, outs),
        scratch_shapes=scratch,
        compiler_params=pltpu.CompilerParams(vmem_limit_bytes=LIMIT),
        cost_estimate=pl.CostEstimate(flops=flops, transcendentals=0, bytes_accessed=0)
        if flops
        else None,
    )(
        *(
            a if a.dtype == jnp.int32 else pltpu.with_memory_space_constraint(a, source)
            for a in args
        )
    )


def gelu_tanh(value):
    return 0.5 * value * (1.0 + jnp.tanh(gelu_scale * (value + gelu_cubic * value * value * value)))


def gelu_slope(value):
    inner = jnp.tanh(gelu_scale * (value + gelu_cubic * value * value * value))
    return 0.5 * (1.0 + inner) + 0.5 * value * (1.0 - inner * inner) * gelu_scale * (
        1.0 + 3.0 * gelu_cubic * value * value
    )


def dot_nn(left, right):
    return jnp.dot(left, right, preferred_element_type=F32)


def dot_nt(left, right):
    return lax.dot_general(left, right, (((1,), (1,)), ((), ())), preferred_element_type=F32)


def mean_row(value):
    return jnp.mean(value, axis=-1, keepdims=True)


def halves(core_ref, width):
    core = core_ref[0]
    return (
        pl.ds(pl.multiple_of(core * width, 128), width),
        pl.ds(pl.multiple_of((1 - core) * width, 128), width),
    )


def spread(value, out):
    for chip in range(out.shape[0]):
        out[chip] = value


def load_kernel(clean, corrupt, own_clean, own_corrupt, sems):
    copies = [
        pltpu.make_async_copy(clean, own_clean, sems.at[0]),
        pltpu.make_async_copy(corrupt, own_corrupt, sems.at[1]),
    ]
    for copy in copies:
        copy.start()
    for copy in copies:
        copy.wait()


def gains_kernel(pre, post, final, out):
    for i, gain in enumerate((pre, post, final)):
        out[i : i + 1] = gain[...].reshape(1, gain.shape[0])


def chip_rows_kernel(where, clean, corrupt, other_clean, other_corrupt, out, stream, rows):
    first = where[0] == 0
    mine, _ = halves(where, out.shape[2])
    for i, (a, b) in enumerate(((clean, other_clean), (corrupt, other_corrupt))):
        a, b = a[...].astype(F32), b[...].astype(F32)
        rows[2 * i : 2 * i + 1] = jnp.where(first, a, b)
        rows[2 * i + 1 : 2 * i + 2] = jnp.where(first, b, a)
    stream[...] = rows[0:2]
    spread(rows[:, mine].astype(BF16), out)


def rows_kernel(pieces, *refs):
    clean, corrupt = refs[-2:]
    clean[...] = pieces[:, :2].reshape(clean.shape)
    corrupt[...] = pieces[:, 2:].reshape(corrupt.shape)


def forward_kernel(where, own, other, w_gate, w_up, w_down, gain, send, hidden, gate, up):
    width = own.shape[1]
    _, theirs = halves(where, width)
    total = 0.0
    for ref in (own, other):
        for at in range(0, width, CHUNK):
            part = ref[:, at : at + CHUNK].astype(F32)
            total = total + jnp.sum(part * part, axis=-1, keepdims=True)
    inv = lax.rsqrt(total / (2 * width) + epsilon)
    gate_pre, up_proj = None, None
    for base, ref in ((where[0], own), (1 - where[0], other)):
        for at in range(0, width, CHUNK):
            lanes = pl.ds(pl.multiple_of(base * width + at, 128), CHUNK)
            part = ref[:, at : at + CHUNK].astype(F32)
            part = (part * inv * gain[0:1, lanes]).astype(BF16)
            g, u = dot_nt(w_gate[:, lanes], part), dot_nt(w_up[:, lanes], part)
            gate_pre = g if gate_pre is None else gate_pre + g
            up_proj = u if up_proj is None else up_proj + u
    gate[...] = gate_pre
    up[...] = up_proj
    act = (gelu_tanh(gate_pre) * up_proj).T.astype(BF16)
    hidden[...] = act
    send[...] = dot_nn(act, w_down[:, theirs]).astype(BF16)


def forward_own_kernel(where, hidden, w_down, out):
    mine, _ = halves(where, out.shape[1])
    out[...] = dot_nn(hidden[...], w_down[:, mine])


def chip_sum_kernel(own, arrived, out):
    out[...] = (own[...] + arrived[...].astype(F32)).astype(BF16).reshape(out.shape)


def total_kernel(pieces, out):
    rows = pieces.shape[0] * pieces.shape[1]
    token = lax.broadcasted_iota(jnp.int32, (8, rows), 0)
    source = lax.broadcasted_iota(jnp.int32, (8, rows), 1)
    pick = (source % 2 == token).astype(F32).astype(BF16)
    out[...] = dot_nn(pick, pieces[...].reshape(rows, out.shape[1]))[: out.shape[0]]


def joined(where, own, other, out):
    mine, theirs = halves(where, own.shape[1])
    out[:, mine] = own[...]
    out[:, theirs] = other[...]
    return out[...]


def wanted_kernel(where, answers, unembed, gains, out):
    lanes = lax.broadcasted_iota(jnp.int32, (1, unembed.shape[0]), 1)
    rows = []
    for core in range(2):
        token = where[1 + core]
        rows.append(
            (lanes == answers[0, token]).astype(F32) - (lanes == answers[1, token]).astype(F32)
        )
    selector = jnp.concatenate(rows * 4, axis=0).astype(BF16)
    out[...] = gains[2:3] * dot_nn(selector, unembed[...])[:2]


def output_kernel(
    where, own, other, stream, weighted, gains, out, grad_output, whole
):
    mine, _ = halves(where, out.shape[2])
    post_gain = gains[1:2]
    mlp_out = joined(where, own, other, whole)
    inv_post = lax.rsqrt(mean_row(mlp_out * mlp_out) + epsilon)
    output = stream[...] + mlp_out * inv_post * post_gain
    inv_final = lax.rsqrt(mean_row(output * output) + epsilon)
    wanted = weighted[...]
    grad_out = inv_final * wanted - output * (inv_final * inv_final * inv_final) * mean_row(
        wanted * output
    )
    grad_output[...] = grad_out
    post_grad = post_gain * grad_out
    whole[...] = inv_post * post_grad - mlp_out * (inv_post * inv_post * inv_post) * mean_row(
        post_grad * mlp_out
    )
    spread(whole[:, mine].astype(BF16), out)


def backward_own_half_kernel(where, own, w_down, out):
    mine, _ = halves(where, own.shape[2])
    out[...] = dot_nt(w_down[:, mine], own[...].reshape(out.shape[1], own.shape[2]))


def backward_kernel(
    where, own_part, other, gate, up, w_gate, w_up, w_down, send, grad_gate, grad_up
):
    width = other.shape[2]
    _, theirs = halves(where, width)
    grad_hidden = own_part[...] + dot_nt(
        w_down[:, theirs], other[...].reshape(own_part.shape[1], width)
    )
    gate_pre = gate[...]
    to_gate = (grad_hidden * up[...] * gelu_slope(gate_pre)).T.astype(BF16)
    to_up = (grad_hidden * gelu_tanh(gate_pre)).T.astype(BF16)
    grad_gate[...] = to_gate
    grad_up[...] = to_up
    send[...] = (dot_nn(to_gate, w_gate[:, theirs]) + dot_nn(to_up, w_up[:, theirs])).astype(BF16)


def backward_own_kernel(where, grad_gate, grad_up, w_gate, w_up, out):
    mine, _ = halves(where, out.shape[1])
    out[...] = dot_nn(grad_gate[...], w_gate[:, mine]) + dot_nn(grad_up[...], w_up[:, mine])


def input_kernel(where, own, other, stream, grad_output, gains, out, whole):
    mine, _ = halves(where, out.shape[2])
    rows = stream[...]
    inv_pre = lax.rsqrt(mean_row(rows * rows) + epsilon)
    pre_grad = gains[0:1] * joined(where, own, other, whole)
    whole[...] = (
        grad_output[...]
        + inv_pre * pre_grad
        - rows * (inv_pre * inv_pre * inv_pre) * mean_row(pre_grad * rows)
    )
    spread(whole[:, mine].astype(BF16), out)


def code_of(where, own, other, w_enc, b_enc):
    first, second = halves(where, own.shape[1])
    return jax.nn.relu(
        dot_nn(own[...], w_enc[first, :]) + dot_nn(other[...], w_enc[second, :]) + b_enc[...]
    )


def code_kernel(where, own, other, w_enc, b_enc, out):
    out[...] = code_of(where, own, other, w_enc, b_enc)


def change_kernel(where, own, other, w_enc, b_enc, clean_code, out):
    out[...] = clean_code[...] - code_of(where, own, other, w_enc, b_enc)


def attribution_own_kernel(where, own, w_dec, out):
    mine, _ = halves(where, own.shape[2])
    out[...] = dot_nt(w_dec[:, mine], own[...].reshape(out.shape[1], own.shape[2]))


def attribution_kernel(where, part, other, w_dec, change, out):
    width = other.shape[2]
    _, theirs = halves(where, width)
    projected = part[...] + dot_nt(w_dec[:, theirs], other[...].reshape(part.shape[1], width))
    out[...] = jnp.sum(change[...] * projected.T, axis=0, keepdims=True)


def exchanged(blocks):
    return lax.all_to_all(blocks, CHIPS, 0, 0, tiled=True)


def swapped(value):
    return lax.ppermute(value, "core", SWAP)


def local(
    resid_clean,
    resid_corrupt,
    answer_ids,
    unembed,
    pre_gain,
    post_gain,
    final_gain,
    w_gate,
    w_up,
    w_down,
    w_enc,
    b_enc,
    w_dec,
):
    width = resid_clean.shape[1]
    half = width // 2
    chips, plane = lax.axis_size(CHIPS), lax.axis_size(("x", "z"))
    tokens = 2 * chips
    core_index = lax.axis_index("core")
    pair = (
        lax.axis_index("y_lo") * (4 * plane)
        + lax.axis_index("y_hi") * plane
        + lax.axis_index(("x", "z"))
    )
    where = jnp.stack([core_index, pair, pair + 2 * plane]).astype(jnp.int32)
    hidden_units, latents = w_gate.shape[1], w_enc.shape[1]
    w_gate, w_up = w_gate.T, w_up.T
    b_enc = b_enc[None]

    halved = shape((tokens, half), BF16)
    halved32 = shape((tokens, half), F32)
    pairs = shape((chips, 2, half), BF16)
    pair_rows = shape((2, width), F32)
    pair_half = shape((2, half), F32)
    units = shape((tokens, hidden_units), BF16)
    units32 = shape((hidden_units, tokens), F32)
    codes = shape((tokens, latents), F32)
    whole = pltpu.VMEM((2, width), F32)

    partner = (swapped(resid_clean), swapped(resid_corrupt))
    one_row = shape((1, width), BF16)
    held = call(
        load_kernel,
        (one_row, one_row),
        resid_clean, resid_corrupt,
        source=pltpu.HBM,
        scratch=[pltpu.SemaphoreType.DMA((2,))],
    )
    *partner, where, clean, corrupt = lax.optimization_barrier((*partner, where, *held))
    quads, stream = call(
        chip_rows_kernel,
        (shape((chips, 4, half), BF16), pair_rows),
        where, clean, corrupt, *partner,
        scratch=[pltpu.VMEM((4, width), F32)],
        flops=HINT,
    )
    own, own_corrupt = call(
        rows_kernel,
        (halved, halved),
        exchanged(quads), w_enc, w_gate, w_up, w_down, unembed, pre_gain, post_gain, final_gain,
        flops=HINT,
    )
    pre_gain, own_corrupt = lax.optimization_barrier((pre_gain, own_corrupt))
    gains = call(gains_kernel, shape((3, width), F32), pre_gain, post_gain, final_gain)
    weighted = call(wanted_kernel, pair_rows, where, answer_ids.T, unembed, gains)
    other = swapped(own)
    other, own_corrupt, gains, weighted = lax.optimization_barrier(
        (other, own_corrupt, gains, weighted)
    )
    other_corrupt = swapped(own_corrupt)

    sent, hidden, gate, up = call(
        forward_kernel,
        (halved, units, units32, units32),
        where, own, other, w_gate, w_up, w_down, gains,
    )
    sent, other_corrupt = lax.optimization_barrier((sent, other_corrupt))
    arrived = swapped(sent)
    own_sum = call(forward_own_kernel, halved32, where, hidden, w_down)
    arrived, own_sum = lax.optimization_barrier((arrived, own_sum))
    own_mlp = call(
        total_kernel, pair_half, exchanged(call(chip_sum_kernel, pairs, own_sum, arrived))
    )
    own_mlp, own = lax.optimization_barrier((own_mlp, own))
    other_mlp = swapped(own_mlp)
    clean_code = call(code_kernel, codes, where, own, other, w_enc, b_enc)
    other_mlp, clean_code = lax.optimization_barrier((other_mlp, clean_code))
    spread_grad, grad_output = call(
        output_kernel,
        (pairs, pair_rows),
        where, own_mlp, other_mlp, stream, weighted, gains,
        scratch=[whole],
    )

    grad_own = exchanged(spread_grad)
    grad_other = swapped(grad_own)
    own_part = call(backward_own_half_kernel, units32, where, grad_own, w_down)
    grad_other, own_part = lax.optimization_barrier((grad_other, own_part))
    sent, grad_gate, grad_up = call(
        backward_kernel,
        (halved, units, units),
        where, own_part, grad_other, gate, up, w_gate, w_up, w_down,
    )
    arrived = swapped(sent)
    own_sum = call(backward_own_kernel, halved32, where, grad_gate, grad_up, w_gate, w_up)
    arrived, own_sum = lax.optimization_barrier((arrived, own_sum))
    own_normed = call(
        total_kernel, pair_half, exchanged(call(chip_sum_kernel, pairs, own_sum, arrived))
    )
    own_normed, own_corrupt = lax.optimization_barrier((own_normed, own_corrupt))
    other_normed = swapped(own_normed)
    change = call(
        change_kernel, codes, where, own_corrupt, other_corrupt, w_enc, b_enc, clean_code
    )
    other_normed, change = lax.optimization_barrier((other_normed, change))
    spread_stream = call(
        input_kernel,
        pairs,
        where, own_normed, other_normed, stream, grad_output, gains,
        scratch=[whole],
    )

    last_own = exchanged(spread_stream)
    last_other = swapped(last_own)
    own_part = call(
        attribution_own_kernel, shape((latents, tokens), F32), where, last_own, w_dec
    )
    last_other, own_part = lax.optimization_barrier((last_other, own_part))
    return call(
        attribution_kernel,
        shape((1, latents), F32),
        where, own_part, last_other, w_dec, change,
        space=jax.ShapeDtypeStruct,
    )


def solution(mesh):
    fine = Mesh(mesh.devices.reshape(2, 2, 2, 4, 4), DEVICES)
    return jax.shard_map(
        local,
        mesh=fine,
        in_specs=(
            P(DEVICES, None),
            P(DEVICES, None),
            P(),
            P(),
            P(),
            P(),
            P(),
            P(None, DEVICES),
            P(None, DEVICES),
            P(DEVICES, None),
            P(None, DEVICES),
            P(DEVICES),
            P(DEVICES, None),
        ),
        out_specs=P(None, DEVICES),
        check_vma=False,
    )
```

```python
import jax
import jax.numpy as jnp
from jax import lax
from jax.experimental import pallas as pl
from jax.experimental.pallas import tpu as pltpu
from jax.sharding import Mesh
from jax.sharding import PartitionSpec as P

epsilon = 1e-06
gelu_scale = 0.7978845608028654
gelu_cubic = 0.044715

DEVICES = ("y_lo", "core", "y_hi", "x", "z")
CHIPS = ("x", "z", "y_lo", "y_hi")
CORES = ("core", *CHIPS)
SWAP = [(0, 1), (1, 0)]
LIMIT = 16 << 20
HINT = 10**11
CHUNK = 768
F32 = jnp.float32
BF16 = jnp.bfloat16
VMEM = pl.BlockSpec(memory_space=pltpu.VMEM)
SMEM = pl.BlockSpec(memory_space=pltpu.SMEM)


def shape(dims, dtype):
    return jax.ShapeDtypeStruct(dims, dtype)


def call(kernel, outs, *args, space=pltpu.VMEM, scratch=(), flops=0, source=pltpu.VMEM):
    return pl.pallas_call(
        kernel,
        out_shape=jax.tree.map(lambda o: space(o.shape, o.dtype), outs),
        in_specs=[
            SMEM if a.dtype == jnp.int32 else pl.BlockSpec(memory_space=source) for a in args
        ],
        out_specs=jax.tree.map(lambda _: VMEM, outs),
        scratch_shapes=scratch,
        compiler_params=pltpu.CompilerParams(vmem_limit_bytes=LIMIT),
        cost_estimate=pl.CostEstimate(flops=flops, transcendentals=0, bytes_accessed=0)
        if flops
        else None,
    )(
        *(
            a if a.dtype == jnp.int32 else pltpu.with_memory_space_constraint(a, source)
            for a in args
        )
    )


def gelu_tanh(value):
    return 0.5 * value * (1.0 + jnp.tanh(gelu_scale * (value + gelu_cubic * value * value * value)))


def gelu_slope(value):
    inner = jnp.tanh(gelu_scale * (value + gelu_cubic * value * value * value))
    return 0.5 * (1.0 + inner) + 0.5 * value * (1.0 - inner * inner) * gelu_scale * (
        1.0 + 3.0 * gelu_cubic * value * value
    )


def dot_nn(left, right):
    return jnp.dot(left, right, preferred_element_type=F32)


def dot_nt(left, right):
    return lax.dot_general(left, right, (((1,), (1,)), ((), ())), preferred_element_type=F32)


def mean_row(value):
    return jnp.mean(value, axis=-1, keepdims=True)


def halves(core_ref, width):
    core = core_ref[0]
    return (
        pl.ds(pl.multiple_of(core * width, 128), width),
        pl.ds(pl.multiple_of((1 - core) * width, 128), width),
    )


def spread(value, out):
    for chip in range(out.shape[0]):
        out[chip] = value


def load_kernel(clean, corrupt, own_clean, own_corrupt, sems):
    copies = [
        pltpu.make_async_copy(clean, own_clean, sems.at[0]),
        pltpu.make_async_copy(corrupt, own_corrupt, sems.at[1]),
    ]
    for copy in copies:
        copy.start()
    for copy in copies:
        copy.wait()


def gains_kernel(pre, post, final, out):
    for i, gain in enumerate((pre, post, final)):
        out[i : i + 1] = gain[...].reshape(1, gain.shape[0])


def chip_rows_kernel(where, clean, corrupt, other_clean, other_corrupt, out, stream, rows):
    first = where[0] == 0
    mine, _ = halves(where, out.shape[2])
    for i, (a, b) in enumerate(((clean, other_clean), (corrupt, other_corrupt))):
        a, b = a[...].astype(F32), b[...].astype(F32)
        rows[2 * i : 2 * i + 1] = jnp.where(first, a, b)
        rows[2 * i + 1 : 2 * i + 2] = jnp.where(first, b, a)
    stream[...] = rows[0:2]
    spread(rows[:, mine].astype(BF16), out)


def rows_kernel(pieces, *refs):
    clean, corrupt = refs[-2:]
    clean[...] = pieces[:, :2].reshape(clean.shape)
    corrupt[...] = pieces[:, 2:].reshape(corrupt.shape)


def forward_kernel(where, own, other, w_gate, w_up, w_down, gain, send, hidden, gate, up):
    width = own.shape[1]
    _, theirs = halves(where, width)
    total = 0.0
    for ref in (own, other):
        for at in range(0, width, CHUNK):
            part = ref[:, at : at + CHUNK].astype(F32)
            total = total + jnp.sum(part * part, axis=-1, keepdims=True)
    inv = lax.rsqrt(total / (2 * width) + epsilon)
    gate_pre, up_proj = None, None
    for base, ref in ((where[0], own), (1 - where[0], other)):
        for at in range(0, width, CHUNK):
            lanes = pl.ds(pl.multiple_of(base * width + at, 128), CHUNK)
            part = ref[:, at : at + CHUNK].astype(F32)
            part = (part * inv * gain[0:1, lanes]).astype(BF16)
            g, u = dot_nt(w_gate[:, lanes], part), dot_nt(w_up[:, lanes], part)
            gate_pre = g if gate_pre is None else gate_pre + g
            up_proj = u if up_proj is None else up_proj + u
    gate[...] = gate_pre
    up[...] = up_proj
    act = (gelu_tanh(gate_pre) * up_proj).T.astype(BF16)
    hidden[...] = act
    send[...] = dot_nn(act, w_down[:, theirs]).astype(BF16)


def forward_own_kernel(where, hidden, w_down, out):
    mine, _ = halves(where, out.shape[1])
    out[...] = dot_nn(hidden[...], w_down[:, mine])


def chip_sum_kernel(own, arrived, out):
    width = out.shape[3]
    for core in range(2):
        part = slice(core * width, (core + 1) * width)
        total = own[:, part] + arrived[:, part].astype(F32)
        out[core] = total.astype(BF16).reshape(out.shape[1:])


def total_kernel(pieces, out):
    rows = pieces.shape[1] * pieces.shape[2]
    width = pieces.shape[3]
    token = lax.broadcasted_iota(jnp.int32, (8, rows), 0)
    source = lax.broadcasted_iota(jnp.int32, (8, rows), 1)
    pick = (source % 2 == token).astype(F32).astype(BF16)
    for core in range(2):
        part = dot_nn(pick, pieces[core].reshape(rows, width))
        out[:, core * width : (core + 1) * width] = part[: out.shape[0]]


def joined(where, own, other, out):
    width = own.shape[1] // 2
    for core, ref in ((where[0], own), (1 - where[0], other)):
        for i in range(2):
            out[:, quarter(2 * i + core, width)] = ref[:, i * width : (i + 1) * width]
    return out[...]


def quarter(index, width):
    return pl.ds(pl.multiple_of(index * width, 128), width)


def spread_quarters(where, whole, out):
    width = out.shape[3]
    for core in range(2):
        value = whole[:, quarter(2 * core + where[0], width)].astype(BF16)
        for chip in range(out.shape[1]):
            out[core, chip] = value


def token_rows(pieces):
    rows = pieces.shape[1] * pieces.shape[2]
    return jnp.concatenate([pieces[i].reshape(rows, pieces.shape[3]) for i in range(2)], axis=1)


def wanted_kernel(where, answers, unembed, gains, out):
    lanes = lax.broadcasted_iota(jnp.int32, (1, unembed.shape[0]), 1)
    rows = []
    for core in range(2):
        token = where[1 + core]
        rows.append(
            (lanes == answers[0, token]).astype(F32) - (lanes == answers[1, token]).astype(F32)
        )
    selector = jnp.concatenate(rows * 4, axis=0).astype(BF16)
    out[...] = gains[2:3] * dot_nn(selector, unembed[...])[:2]


def output_kernel(
    where, own, other, stream, weighted, gains, out, grad_output, whole
):
    post_gain = gains[1:2]
    mlp_out = joined(where, own, other, whole)
    inv_post = lax.rsqrt(mean_row(mlp_out * mlp_out) + epsilon)
    output = stream[...] + mlp_out * inv_post * post_gain
    inv_final = lax.rsqrt(mean_row(output * output) + epsilon)
    wanted = weighted[...]
    grad_out = inv_final * wanted - output * (inv_final * inv_final * inv_final) * mean_row(
        wanted * output
    )
    grad_output[...] = grad_out
    post_grad = post_gain * grad_out
    whole[...] = inv_post * post_grad - mlp_out * (inv_post * inv_post * inv_post) * mean_row(
        post_grad * mlp_out
    )
    spread_quarters(where, whole, out)


def backward_own_half_kernel(where, own, w_down, out):
    mine, _ = halves(where, 2 * own.shape[3])
    out[...] = dot_nt(w_down[:, mine], token_rows(own))


def backward_kernel(
    where, own_part, other, gate, up, w_gate, w_up, w_down, send, grad_gate, grad_up
):
    _, theirs = halves(where, 2 * other.shape[3])
    grad_hidden = own_part[...] + dot_nt(w_down[:, theirs], token_rows(other))
    gate_pre = gate[...]
    to_gate = (grad_hidden * up[...] * gelu_slope(gate_pre)).T.astype(BF16)
    to_up = (grad_hidden * gelu_tanh(gate_pre)).T.astype(BF16)
    grad_gate[...] = to_gate
    grad_up[...] = to_up
    send[...] = (dot_nn(to_gate, w_gate[:, theirs]) + dot_nn(to_up, w_up[:, theirs])).astype(BF16)


def backward_own_kernel(where, grad_gate, grad_up, w_gate, w_up, out):
    mine, _ = halves(where, out.shape[1])
    out[...] = dot_nn(grad_gate[...], w_gate[:, mine]) + dot_nn(grad_up[...], w_up[:, mine])


def input_kernel(where, own, other, stream, grad_output, gains, out, whole):
    rows = stream[...]
    inv_pre = lax.rsqrt(mean_row(rows * rows) + epsilon)
    pre_grad = gains[0:1] * joined(where, own, other, whole)
    whole[...] = (
        grad_output[...]
        + inv_pre * pre_grad
        - rows * (inv_pre * inv_pre * inv_pre) * mean_row(pre_grad * rows)
    )
    spread_quarters(where, whole, out)


def code_of(where, own, other, w_enc, b_enc):
    first, second = halves(where, own.shape[1])
    return jax.nn.relu(
        dot_nn(own[...], w_enc[first, :]) + dot_nn(other[...], w_enc[second, :]) + b_enc[...]
    )


def code_kernel(where, own, other, w_enc, b_enc, out):
    out[...] = code_of(where, own, other, w_enc, b_enc)


def change_kernel(where, own, other, w_enc, b_enc, clean_code, out):
    out[...] = clean_code[...] - code_of(where, own, other, w_enc, b_enc)


def attribution_own_kernel(where, own, w_dec, out):
    mine, _ = halves(where, 2 * own.shape[3])
    out[...] = dot_nt(w_dec[:, mine], token_rows(own))


def attribution_kernel(where, part, other, w_dec, change, out):
    _, theirs = halves(where, 2 * other.shape[3])
    projected = part[...] + dot_nt(w_dec[:, theirs], token_rows(other))
    out[...] = jnp.sum(change[...] * projected.T, axis=0, keepdims=True)


def exchanged(blocks):
    return lax.all_to_all(blocks, CHIPS, 0, 0, tiled=True)


def exchanged_by_core(blocks):
    flat = blocks.reshape(-1, *blocks.shape[2:])
    return lax.all_to_all(flat, CORES, 0, 0, tiled=True).reshape(blocks.shape)


def swapped(value):
    return lax.ppermute(value, "core", SWAP)


def local(
    resid_clean,
    resid_corrupt,
    answer_ids,
    unembed,
    pre_gain,
    post_gain,
    final_gain,
    w_gate,
    w_up,
    w_down,
    w_enc,
    b_enc,
    w_dec,
):
    width = resid_clean.shape[1]
    half = width // 2
    chips, plane = lax.axis_size(CHIPS), lax.axis_size(("x", "z"))
    tokens = 2 * chips
    core_index = lax.axis_index("core")
    pair = (
        lax.axis_index("y_lo") * (4 * plane)
        + lax.axis_index("y_hi") * plane
        + lax.axis_index(("x", "z"))
    )
    where = jnp.stack([core_index, pair, pair + 2 * plane]).astype(jnp.int32)
    hidden_units, latents = w_gate.shape[1], w_enc.shape[1]
    w_gate, w_up = w_gate.T, w_up.T
    b_enc = b_enc[None]

    halved = shape((tokens, half), BF16)
    halved32 = shape((tokens, half), F32)
    pairs = shape((2, chips, 2, half // 2), BF16)
    pair_rows = shape((2, width), F32)
    pair_half = shape((2, half), F32)
    units = shape((tokens, hidden_units), BF16)
    units32 = shape((hidden_units, tokens), F32)
    codes = shape((tokens, latents), F32)
    whole = pltpu.VMEM((2, width), F32)

    partner = (swapped(resid_clean), swapped(resid_corrupt))
    one_row = shape((1, width), BF16)
    held = call(
        load_kernel,
        (one_row, one_row),
        resid_clean, resid_corrupt,
        source=pltpu.HBM,
        scratch=[pltpu.SemaphoreType.DMA((2,))],
    )
    *partner, where, clean, corrupt = lax.optimization_barrier((*partner, where, *held))
    quads, stream = call(
        chip_rows_kernel,
        (shape((chips, 4, half), BF16), pair_rows),
        where, clean, corrupt, *partner,
        scratch=[pltpu.VMEM((4, width), F32)],
        flops=HINT,
    )
    own, own_corrupt = call(
        rows_kernel,
        (halved, halved),
        exchanged(quads), w_enc, w_gate, w_up, w_down, unembed, pre_gain, post_gain, final_gain,
        flops=HINT,
    )
    pre_gain, own_corrupt = lax.optimization_barrier((pre_gain, own_corrupt))
    gains = call(gains_kernel, shape((3, width), F32), pre_gain, post_gain, final_gain)
    weighted = call(wanted_kernel, pair_rows, where, answer_ids.T, unembed, gains)
    other = swapped(own)
    other, own_corrupt, gains, weighted = lax.optimization_barrier(
        (other, own_corrupt, gains, weighted)
    )
    other_corrupt = swapped(own_corrupt)

    sent, hidden, gate, up = call(
        forward_kernel,
        (halved, units, units32, units32),
        where, own, other, w_gate, w_up, w_down, gains,
    )
    sent, other_corrupt = lax.optimization_barrier((sent, other_corrupt))
    arrived = swapped(sent)
    own_sum = call(forward_own_kernel, halved32, where, hidden, w_down)
    arrived, own_sum = lax.optimization_barrier((arrived, own_sum))
    own_mlp = call(
        total_kernel, pair_half, exchanged_by_core(call(chip_sum_kernel, pairs, own_sum, arrived))
    )
    own_mlp, own = lax.optimization_barrier((own_mlp, own))
    other_mlp = swapped(own_mlp)
    clean_code = call(code_kernel, codes, where, own, other, w_enc, b_enc)
    other_mlp, clean_code = lax.optimization_barrier((other_mlp, clean_code))
    spread_grad, grad_output = call(
        output_kernel,
        (pairs, pair_rows),
        where, own_mlp, other_mlp, stream, weighted, gains,
        scratch=[whole],
    )

    grad_own = exchanged_by_core(spread_grad)
    grad_other = swapped(grad_own)
    own_part = call(backward_own_half_kernel, units32, where, grad_own, w_down)
    grad_other, own_part = lax.optimization_barrier((grad_other, own_part))
    sent, grad_gate, grad_up = call(
        backward_kernel,
        (halved, units, units),
        where, own_part, grad_other, gate, up, w_gate, w_up, w_down,
    )
    arrived = swapped(sent)
    own_sum = call(backward_own_kernel, halved32, where, grad_gate, grad_up, w_gate, w_up)
    arrived, own_sum = lax.optimization_barrier((arrived, own_sum))
    own_normed = call(
        total_kernel, pair_half, exchanged_by_core(call(chip_sum_kernel, pairs, own_sum, arrived))
    )
    own_normed, own_corrupt = lax.optimization_barrier((own_normed, own_corrupt))
    other_normed = swapped(own_normed)
    change = call(
        change_kernel, codes, where, own_corrupt, other_corrupt, w_enc, b_enc, clean_code
    )
    other_normed, change = lax.optimization_barrier((other_normed, change))
    spread_stream = call(
        input_kernel,
        pairs,
        where, own_normed, other_normed, stream, grad_output, gains,
        scratch=[whole],
    )

    last_own = exchanged_by_core(spread_stream)
    last_other = swapped(last_own)
    own_part = call(
        attribution_own_kernel, shape((latents, tokens), F32), where, last_own, w_dec
    )
    last_other, own_part = lax.optimization_barrier((last_other, own_part))
    return call(
        attribution_kernel,
        shape((1, latents), F32),
        where, own_part, last_other, w_dec, change,
        space=jax.ShapeDtypeStruct,
    )


def solution(mesh):
    fine = Mesh(mesh.devices.reshape(2, 2, 2, 4, 4), DEVICES)
    return jax.shard_map(
        local,
        mesh=fine,
        in_specs=(
            P(DEVICES, None),
            P(DEVICES, None),
            P(),
            P(),
            P(),
            P(),
            P(),
            P(None, DEVICES),
            P(None, DEVICES),
            P(DEVICES, None),
            P(None, DEVICES),
            P(DEVICES),
            P(DEVICES, None),
        ),
        out_specs=P(None, DEVICES),
        check_vma=False,
    )
```

```python
import jax
import jax.numpy as jnp
from jax import lax
from jax.experimental import pallas as pl
from jax.experimental.pallas import tpu as pltpu
from jax.sharding import Mesh
from jax.sharding import PartitionSpec as P

epsilon = 1e-06
gelu_scale = 0.7978845608028654
gelu_cubic = 0.044715

DEVICES = ("y_lo", "core", "y_hi", "x", "z")
CHIPS = ("y_hi", "z", "y_lo", "x")
CORES = (*CHIPS, "core")
SWAP = [(0, 1), (1, 0)]
LIMIT = 16 << 20
HINT = 10**11
CHUNK = 768
F32 = jnp.float32
BF16 = jnp.bfloat16
VMEM = pl.BlockSpec(memory_space=pltpu.VMEM)
SMEM = pl.BlockSpec(memory_space=pltpu.SMEM)


def shape(dims, dtype):
    return jax.ShapeDtypeStruct(dims, dtype)


def call(kernel, outs, *args, space=pltpu.VMEM, scratch=(), flops=0, source=pltpu.VMEM):
    return pl.pallas_call(
        kernel,
        out_shape=jax.tree.map(lambda o: space(o.shape, o.dtype), outs),
        in_specs=[
            SMEM if a.dtype == jnp.int32 else pl.BlockSpec(memory_space=source) for a in args
        ],
        out_specs=jax.tree.map(lambda _: VMEM, outs),
        scratch_shapes=scratch,
        compiler_params=pltpu.CompilerParams(vmem_limit_bytes=LIMIT),
        cost_estimate=pl.CostEstimate(flops=flops, transcendentals=0, bytes_accessed=0)
        if flops
        else None,
    )(
        *(
            a if a.dtype == jnp.int32 else pltpu.with_memory_space_constraint(a, source)
            for a in args
        )
    )


def gelu_tanh(value):
    return 0.5 * value * (1.0 + jnp.tanh(gelu_scale * (value + gelu_cubic * value * value * value)))


def gelu_slope(value):
    inner = jnp.tanh(gelu_scale * (value + gelu_cubic * value * value * value))
    return 0.5 * (1.0 + inner) + 0.5 * value * (1.0 - inner * inner) * gelu_scale * (
        1.0 + 3.0 * gelu_cubic * value * value
    )


def dot_nn(left, right):
    return jnp.dot(left, right, preferred_element_type=F32)


def dot_nt(left, right):
    return lax.dot_general(left, right, (((1,), (1,)), ((), ())), preferred_element_type=F32)


def mean_row(value):
    return jnp.mean(value, axis=-1, keepdims=True)


def halves(core_ref, width):
    core = core_ref[0]
    return (
        pl.ds(pl.multiple_of(core * width, 128), width),
        pl.ds(pl.multiple_of((1 - core) * width, 128), width),
    )


def spread(value, out):
    for chip in range(out.shape[0]):
        out[chip] = value


def load_kernel(clean, corrupt, own_clean, own_corrupt, sems):
    copies = [
        pltpu.make_async_copy(clean, own_clean, sems.at[0]),
        pltpu.make_async_copy(corrupt, own_corrupt, sems.at[1]),
    ]
    for copy in copies:
        copy.start()
    for copy in copies:
        copy.wait()


def gains_kernel(pre, post, final, out):
    for i, gain in enumerate((pre, post, final)):
        out[i : i + 1] = gain[...].reshape(1, gain.shape[0])


def chip_rows_kernel(where, clean, corrupt, other_clean, other_corrupt, out, stream, rows):
    first = where[0] == 0
    mine, _ = halves(where, out.shape[2])
    for i, (a, b) in enumerate(((clean, other_clean), (corrupt, other_corrupt))):
        a, b = a[...].astype(F32), b[...].astype(F32)
        rows[2 * i : 2 * i + 1] = jnp.where(first, a, b)
        rows[2 * i + 1 : 2 * i + 2] = jnp.where(first, b, a)
    stream[...] = rows[0:2]
    spread(rows[:, mine].astype(BF16), out)


def rows_kernel(pieces, *refs):
    clean, corrupt = refs[-2:]
    clean[...] = pieces[:, :2].reshape(clean.shape)
    corrupt[...] = pieces[:, 2:].reshape(corrupt.shape)


def forward_kernel(where, own, other, w_gate, w_up, w_down, gain, send, hidden, gate, up):
    width = own.shape[1]
    _, theirs = halves(where, width)
    total = 0.0
    for ref in (own, other):
        for at in range(0, width, CHUNK):
            part = ref[:, at : at + CHUNK].astype(F32)
            total = total + jnp.sum(part * part, axis=-1, keepdims=True)
    inv = lax.rsqrt(total / (2 * width) + epsilon)
    gate_pre, up_proj = None, None
    for base, ref in ((where[0], own), (1 - where[0], other)):
        for at in range(0, width, CHUNK):
            lanes = pl.ds(pl.multiple_of(base * width + at, 128), CHUNK)
            part = ref[:, at : at + CHUNK].astype(F32)
            part = (part * inv * gain[0:1, lanes]).astype(BF16)
            g, u = dot_nt(w_gate[:, lanes], part), dot_nt(w_up[:, lanes], part)
            gate_pre = g if gate_pre is None else gate_pre + g
            up_proj = u if up_proj is None else up_proj + u
    gate[...] = gate_pre
    up[...] = up_proj
    act = (gelu_tanh(gate_pre) * up_proj).T.astype(BF16)
    hidden[...] = act
    send[...] = dot_nn(act, w_down[:, theirs]).astype(BF16)


def forward_own_kernel(where, hidden, w_down, out):
    mine, _ = halves(where, out.shape[1])
    out[...] = dot_nn(hidden[...], w_down[:, mine])


def chip_sum_kernel(own, arrived, out):
    width = out.shape[3]
    for core in range(2):
        part = slice(core * width, (core + 1) * width)
        total = own[:, part] + arrived[:, part].astype(F32)
        out[:, core] = total.astype(BF16).reshape(out.shape[0], 2, width)


def total_kernel(pieces, out):
    rows = pieces.shape[0] * pieces.shape[2]
    width = pieces.shape[3]
    token = lax.broadcasted_iota(jnp.int32, (8, rows), 0)
    source = lax.broadcasted_iota(jnp.int32, (8, rows), 1)
    pick = (source % 2 == token).astype(F32).astype(BF16)
    for core in range(2):
        part = dot_nn(pick, pieces[:, core].reshape(rows, width))
        out[:, core * width : (core + 1) * width] = part[: out.shape[0]]


def joined(where, own, other, out):
    width = own.shape[1] // 2
    for core, ref in ((where[0], own), (1 - where[0], other)):
        for i in range(2):
            out[:, quarter(2 * i + core, width)] = ref[:, i * width : (i + 1) * width]
    return out[...]


def quarter(index, width):
    return pl.ds(pl.multiple_of(index * width, 128), width)


def spread_quarters(where, whole, out):
    width = out.shape[3]
    for core in range(2):
        value = whole[:, quarter(2 * core + where[0], width)].astype(BF16)
        for chip in range(out.shape[0]):
            out[chip, core] = value


def token_rows(pieces):
    rows = pieces.shape[0] * pieces.shape[2]
    return jnp.concatenate([pieces[:, i].reshape(rows, pieces.shape[3]) for i in range(2)], axis=1)


def wanted_kernel(where, answers, unembed, gains, out):
    lanes = lax.broadcasted_iota(jnp.int32, (1, unembed.shape[0]), 1)
    rows = []
    for core in range(2):
        token = where[1 + core]
        rows.append(
            (lanes == answers[0, token]).astype(F32) - (lanes == answers[1, token]).astype(F32)
        )
    selector = jnp.concatenate(rows * 4, axis=0).astype(BF16)
    out[...] = gains[2:3] * dot_nn(selector, unembed[...])[:2]


def output_kernel(
    where, own, other, stream, weighted, gains, out, grad_output, whole
):
    post_gain = gains[1:2]
    mlp_out = joined(where, own, other, whole)
    inv_post = lax.rsqrt(mean_row(mlp_out * mlp_out) + epsilon)
    output = stream[...] + mlp_out * inv_post * post_gain
    inv_final = lax.rsqrt(mean_row(output * output) + epsilon)
    wanted = weighted[...]
    grad_out = inv_final * wanted - output * (inv_final * inv_final * inv_final) * mean_row(
        wanted * output
    )
    grad_output[...] = grad_out
    post_grad = post_gain * grad_out
    whole[...] = inv_post * post_grad - mlp_out * (inv_post * inv_post * inv_post) * mean_row(
        post_grad * mlp_out
    )
    spread_quarters(where, whole, out)


def backward_own_half_kernel(where, own, w_down, out):
    mine, _ = halves(where, 2 * own.shape[3])
    out[...] = dot_nt(w_down[:, mine], token_rows(own))


def backward_kernel(
    where, own_part, other, gate, up, w_gate, w_up, w_down, send, grad_gate, grad_up
):
    _, theirs = halves(where, 2 * other.shape[3])
    grad_hidden = own_part[...] + dot_nt(w_down[:, theirs], token_rows(other))
    gate_pre = gate[...]
    to_gate = (grad_hidden * up[...] * gelu_slope(gate_pre)).T.astype(BF16)
    to_up = (grad_hidden * gelu_tanh(gate_pre)).T.astype(BF16)
    grad_gate[...] = to_gate
    grad_up[...] = to_up
    send[...] = (dot_nn(to_gate, w_gate[:, theirs]) + dot_nn(to_up, w_up[:, theirs])).astype(BF16)


def backward_own_kernel(where, grad_gate, grad_up, w_gate, w_up, out):
    mine, _ = halves(where, out.shape[1])
    out[...] = dot_nn(grad_gate[...], w_gate[:, mine]) + dot_nn(grad_up[...], w_up[:, mine])


def input_kernel(where, own, other, stream, grad_output, gains, out, whole):
    rows = stream[...]
    inv_pre = lax.rsqrt(mean_row(rows * rows) + epsilon)
    pre_grad = gains[0:1] * joined(where, own, other, whole)
    whole[...] = (
        grad_output[...]
        + inv_pre * pre_grad
        - rows * (inv_pre * inv_pre * inv_pre) * mean_row(pre_grad * rows)
    )
    spread_quarters(where, whole, out)


def code_of(where, own, other, w_enc, b_enc):
    first, second = halves(where, own.shape[1])
    return jax.nn.relu(
        dot_nn(own[...], w_enc[first, :]) + dot_nn(other[...], w_enc[second, :]) + b_enc[...]
    )


def code_kernel(where, own, other, w_enc, b_enc, out):
    out[...] = code_of(where, own, other, w_enc, b_enc)


def change_kernel(where, own, other, w_enc, b_enc, clean_code, out):
    out[...] = clean_code[...] - code_of(where, own, other, w_enc, b_enc)


def attribution_own_kernel(where, own, w_dec, out):
    mine, _ = halves(where, 2 * own.shape[3])
    out[...] = dot_nt(w_dec[:, mine], token_rows(own))


def attribution_kernel(where, part, other, w_dec, change, out):
    _, theirs = halves(where, 2 * other.shape[3])
    projected = part[...] + dot_nt(w_dec[:, theirs], token_rows(other))
    out[...] = jnp.sum(change[...] * projected.T, axis=0, keepdims=True)


def exchanged(blocks):
    return lax.all_to_all(blocks, CHIPS, 0, 0, tiled=True)


def exchanged_by_core(blocks):
    flat = blocks.reshape(-1, *blocks.shape[2:])
    return lax.all_to_all(flat, CORES, 0, 0, tiled=True).reshape(blocks.shape)


def swapped(value):
    return lax.ppermute(value, "core", SWAP)


def local(
    resid_clean,
    resid_corrupt,
    answer_ids,
    unembed,
    pre_gain,
    post_gain,
    final_gain,
    w_gate,
    w_up,
    w_down,
    w_enc,
    b_enc,
    w_dec,
):
    width = resid_clean.shape[1]
    half = width // 2
    chips, plane = lax.axis_size(CHIPS), lax.axis_size(("x", "z"))
    tokens = 2 * chips
    core_index = lax.axis_index("core")
    pair = (
        lax.axis_index("y_lo") * (4 * plane)
        + lax.axis_index("y_hi") * plane
        + lax.axis_index(("x", "z"))
    )
    where = jnp.stack([core_index, pair, pair + 2 * plane]).astype(jnp.int32)
    hidden_units, latents = w_gate.shape[1], w_enc.shape[1]
    w_gate, w_up = w_gate.T, w_up.T
    b_enc = b_enc[None]

    halved = shape((tokens, half), BF16)
    halved32 = shape((tokens, half), F32)
    pairs = shape((chips, 2, 2, half // 2), BF16)
    pair_rows = shape((2, width), F32)
    pair_half = shape((2, half), F32)
    units = shape((tokens, hidden_units), BF16)
    units32 = shape((hidden_units, tokens), F32)
    codes = shape((tokens, latents), F32)
    whole = pltpu.VMEM((2, width), F32)

    partner = (swapped(resid_clean), swapped(resid_corrupt))
    one_row = shape((1, width), BF16)
    held = call(
        load_kernel,
        (one_row, one_row),
        resid_clean, resid_corrupt,
        source=pltpu.HBM,
        scratch=[pltpu.SemaphoreType.DMA((2,))],
    )
    *partner, where, clean, corrupt = lax.optimization_barrier((*partner, where, *held))
    quads, stream = call(
        chip_rows_kernel,
        (shape((chips, 4, half), BF16), pair_rows),
        where, clean, corrupt, *partner,
        scratch=[pltpu.VMEM((4, width), F32)],
        flops=HINT,
    )
    own, own_corrupt = call(
        rows_kernel,
        (halved, halved),
        exchanged(quads), w_enc, w_gate, w_up, w_down, unembed, pre_gain, post_gain, final_gain,
        flops=HINT,
    )
    pre_gain, own_corrupt = lax.optimization_barrier((pre_gain, own_corrupt))
    gains = call(gains_kernel, shape((3, width), F32), pre_gain, post_gain, final_gain)
    weighted = call(wanted_kernel, pair_rows, where, answer_ids.T, unembed, gains)
    other = swapped(own)
    other, own_corrupt, gains, weighted = lax.optimization_barrier(
        (other, own_corrupt, gains, weighted)
    )
    other_corrupt = swapped(own_corrupt)

    sent, hidden, gate, up = call(
        forward_kernel,
        (halved, units, units32, units32),
        where, own, other, w_gate, w_up, w_down, gains,
    )
    sent, other_corrupt = lax.optimization_barrier((sent, other_corrupt))
    arrived = swapped(sent)
    own_sum = call(forward_own_kernel, halved32, where, hidden, w_down)
    arrived, own_sum = lax.optimization_barrier((arrived, own_sum))
    own_mlp = call(
        total_kernel, pair_half, exchanged_by_core(call(chip_sum_kernel, pairs, own_sum, arrived))
    )
    own_mlp, own = lax.optimization_barrier((own_mlp, own))
    other_mlp = swapped(own_mlp)
    clean_code = call(code_kernel, codes, where, own, other, w_enc, b_enc)
    other_mlp, clean_code = lax.optimization_barrier((other_mlp, clean_code))
    spread_grad, grad_output = call(
        output_kernel,
        (pairs, pair_rows),
        where, own_mlp, other_mlp, stream, weighted, gains,
        scratch=[whole],
    )

    grad_own = exchanged_by_core(spread_grad)
    grad_other = swapped(grad_own)
    own_part = call(backward_own_half_kernel, units32, where, grad_own, w_down)
    grad_other, own_part = lax.optimization_barrier((grad_other, own_part))
    sent, grad_gate, grad_up = call(
        backward_kernel,
        (halved, units, units),
        where, own_part, grad_other, gate, up, w_gate, w_up, w_down,
    )
    arrived = swapped(sent)
    own_sum = call(backward_own_kernel, halved32, where, grad_gate, grad_up, w_gate, w_up)
    arrived, own_sum = lax.optimization_barrier((arrived, own_sum))
    own_normed = call(
        total_kernel, pair_half, exchanged_by_core(call(chip_sum_kernel, pairs, own_sum, arrived))
    )
    own_normed, own_corrupt = lax.optimization_barrier((own_normed, own_corrupt))
    other_normed = swapped(own_normed)
    change = call(
        change_kernel, codes, where, own_corrupt, other_corrupt, w_enc, b_enc, clean_code
    )
    other_normed, change = lax.optimization_barrier((other_normed, change))
    spread_stream = call(
        input_kernel,
        pairs,
        where, own_normed, other_normed, stream, grad_output, gains,
        scratch=[whole],
    )

    last_own = exchanged_by_core(spread_stream)
    last_other = swapped(last_own)
    own_part = call(
        attribution_own_kernel, shape((latents, tokens), F32), where, last_own, w_dec
    )
    last_other, own_part = lax.optimization_barrier((last_other, own_part))
    return call(
        attribution_kernel,
        shape((1, latents), F32),
        where, own_part, last_other, w_dec, change,
        space=jax.ShapeDtypeStruct,
    )


def solution(mesh):
    fine = Mesh(mesh.devices.reshape(2, 2, 2, 4, 4), DEVICES)
    return jax.shard_map(
        local,
        mesh=fine,
        in_specs=(
            P(DEVICES, None),
            P(DEVICES, None),
            P(),
            P(),
            P(),
            P(),
            P(),
            P(None, DEVICES),
            P(None, DEVICES),
            P(DEVICES, None),
            P(None, DEVICES),
            P(DEVICES),
            P(DEVICES, None),
        ),
        out_specs=P(None, DEVICES),
        check_vma=False,
    )
```

```python
import jax
import jax.numpy as jnp
from jax import lax
from jax.experimental import pallas as pl
from jax.experimental.pallas import tpu as pltpu
from jax.sharding import Mesh
from jax.sharding import PartitionSpec as P

epsilon = 1e-06
gelu_scale = 0.7978845608028654
gelu_cubic = 0.044715

DEVICES = ("y_lo", "core", "y_hi", "x", "z")
CHIPS = ("y_hi", "z", "y_lo", "x")
CORES = (*CHIPS, "core")
SWAP = [(0, 1), (1, 0)]
LIMIT = 16 << 20
HINT = 10**11
CHUNK = 768
F32 = jnp.float32
BF16 = jnp.bfloat16
VMEM = pl.BlockSpec(memory_space=pltpu.VMEM)
SMEM = pl.BlockSpec(memory_space=pltpu.SMEM)


def shape(dims, dtype):
    return jax.ShapeDtypeStruct(dims, dtype)


def call(kernel, outs, *args, space=pltpu.VMEM, scratch=(), flops=0, source=pltpu.VMEM):
    return pl.pallas_call(
        kernel,
        out_shape=jax.tree.map(lambda o: space(o.shape, o.dtype), outs),
        in_specs=[
            SMEM if a.dtype == jnp.int32 else pl.BlockSpec(memory_space=source) for a in args
        ],
        out_specs=jax.tree.map(lambda _: VMEM, outs),
        scratch_shapes=scratch,
        compiler_params=pltpu.CompilerParams(vmem_limit_bytes=LIMIT),
        cost_estimate=pl.CostEstimate(flops=flops, transcendentals=0, bytes_accessed=0)
        if flops
        else None,
    )(
        *(
            a if a.dtype == jnp.int32 else pltpu.with_memory_space_constraint(a, source)
            for a in args
        )
    )


def gelu_tanh(value):
    return 0.5 * value * (1.0 + jnp.tanh(gelu_scale * (value + gelu_cubic * value * value * value)))


def gelu_slope(value):
    inner = jnp.tanh(gelu_scale * (value + gelu_cubic * value * value * value))
    return 0.5 * (1.0 + inner) + 0.5 * value * (1.0 - inner * inner) * gelu_scale * (
        1.0 + 3.0 * gelu_cubic * value * value
    )


def dot_nn(left, right):
    return jnp.dot(left, right, preferred_element_type=F32)


def dot_nt(left, right):
    return lax.dot_general(left, right, (((1,), (1,)), ((), ())), preferred_element_type=F32)


def mean_row(value):
    return jnp.mean(value, axis=-1, keepdims=True)


def halves(core_ref, width):
    core = core_ref[0]
    return (
        pl.ds(pl.multiple_of(core * width, 128), width),
        pl.ds(pl.multiple_of((1 - core) * width, 128), width),
    )


def load_kernel(clean, corrupt, own_clean, own_corrupt, sems):
    copies = [
        pltpu.make_async_copy(clean, own_clean, sems.at[0]),
        pltpu.make_async_copy(corrupt, own_corrupt, sems.at[1]),
    ]
    for copy in copies:
        copy.start()
    for copy in copies:
        copy.wait()


def gains_kernel(pre, post, final, out):
    for i, gain in enumerate((pre, post, final)):
        out[i : i + 1] = gain[...].reshape(1, gain.shape[0])


def chip_rows_kernel(where, clean, corrupt, other_clean, other_corrupt, out, stream, rows):
    first = where[0] == 0
    for i, (a, b) in enumerate(((clean, other_clean), (corrupt, other_corrupt))):
        a, b = a[...].astype(F32), b[...].astype(F32)
        rows[2 * i : 2 * i + 1] = jnp.where(first, a, b)
        rows[2 * i + 1 : 2 * i + 2] = jnp.where(first, b, a)
    stream[...] = rows[0:2]
    spread_quarters(where, rows, out)


def rows_kernel(pieces, *refs):
    clean, corrupt = refs[-2:]
    width = pieces.shape[3]
    for core in range(2):
        lanes = slice(core * width, (core + 1) * width)
        clean[:, lanes] = pieces[:, core, :2].reshape(clean.shape[0], width)
        corrupt[:, lanes] = pieces[:, core, 2:].reshape(corrupt.shape[0], width)


def forward_kernel(where, own, other, w_gate, w_up, w_down, gain, send, hidden, gate, up):
    width = own.shape[1]
    _, theirs = halves(where, width)
    total = 0.0
    for ref in (own, other):
        for at in range(0, width, CHUNK):
            part = ref[:, at : at + CHUNK].astype(F32)
            total = total + jnp.sum(part * part, axis=-1, keepdims=True)
    inv = lax.rsqrt(total / (2 * width) + epsilon)
    gate_pre, up_proj = None, None
    for base, ref in ((where[0], own), (1 - where[0], other)):
        for at in range(0, width, CHUNK):
            lanes = pl.ds(pl.multiple_of(base * width + at, 128), CHUNK)
            part = ref[:, at : at + CHUNK].astype(F32)
            part = (part * inv * gain[0:1, lanes]).astype(BF16)
            g, u = dot_nt(w_gate[:, lanes], part), dot_nt(w_up[:, lanes], part)
            gate_pre = g if gate_pre is None else gate_pre + g
            up_proj = u if up_proj is None else up_proj + u
    gate[...] = gate_pre
    up[...] = up_proj
    act = (gelu_tanh(gate_pre) * up_proj).T.astype(BF16)
    hidden[...] = act
    send[...] = dot_nn(act, w_down[:, theirs]).astype(BF16)


def forward_own_kernel(where, hidden, w_down, out):
    mine, _ = halves(where, out.shape[1])
    out[...] = dot_nn(hidden[...], w_down[:, mine])


def chip_sum_kernel(own, arrived, out):
    width = out.shape[3]
    for core in range(2):
        part = slice(core * width, (core + 1) * width)
        total = own[:, part] + arrived[:, part].astype(F32)
        out[:, core] = total.astype(BF16).reshape(out.shape[0], 2, width)


def total_kernel(pieces, out):
    rows = pieces.shape[0] * pieces.shape[2]
    width = pieces.shape[3]
    token = lax.broadcasted_iota(jnp.int32, (8, rows), 0)
    source = lax.broadcasted_iota(jnp.int32, (8, rows), 1)
    pick = (source % 2 == token).astype(F32).astype(BF16)
    for core in range(2):
        part = dot_nn(pick, pieces[:, core].reshape(rows, width))
        out[:, core * width : (core + 1) * width] = part[: out.shape[0]]


def joined(where, own, other, out):
    width = own.shape[1] // 2
    for core, ref in ((where[0], own), (1 - where[0], other)):
        for i in range(2):
            out[:, quarter(2 * i + core, width)] = ref[:, i * width : (i + 1) * width]
    return out[...]


def quarter(index, width):
    return pl.ds(pl.multiple_of(index * width, 128), width)


def spread_quarters(where, whole, out):
    width = out.shape[3]
    for core in range(2):
        value = whole[:, quarter(2 * core + where[0], width)].astype(BF16)
        for chip in range(out.shape[0]):
            out[chip, core] = value


def token_rows(pieces):
    rows = pieces.shape[0] * pieces.shape[2]
    return jnp.concatenate([pieces[:, i].reshape(rows, pieces.shape[3]) for i in range(2)], axis=1)


def wanted_kernel(where, answers, unembed, gains, out):
    lanes = lax.broadcasted_iota(jnp.int32, (1, unembed.shape[0]), 1)
    rows = []
    for core in range(2):
        token = where[1 + core]
        rows.append(
            (lanes == answers[0, token]).astype(F32) - (lanes == answers[1, token]).astype(F32)
        )
    selector = jnp.concatenate(rows * 4, axis=0).astype(BF16)
    out[...] = gains[2:3] * dot_nn(selector, unembed[...])[:2]


def output_kernel(
    where, own, other, stream, weighted, gains, out, grad_output, whole
):
    post_gain = gains[1:2]
    mlp_out = joined(where, own, other, whole)
    inv_post = lax.rsqrt(mean_row(mlp_out * mlp_out) + epsilon)
    output = stream[...] + mlp_out * inv_post * post_gain
    inv_final = lax.rsqrt(mean_row(output * output) + epsilon)
    wanted = weighted[...]
    grad_out = inv_final * wanted - output * (inv_final * inv_final * inv_final) * mean_row(
        wanted * output
    )
    grad_output[...] = grad_out
    post_grad = post_gain * grad_out
    whole[...] = inv_post * post_grad - mlp_out * (inv_post * inv_post * inv_post) * mean_row(
        post_grad * mlp_out
    )
    spread_quarters(where, whole, out)


def backward_own_half_kernel(where, own, w_down, out):
    mine, _ = halves(where, 2 * own.shape[3])
    out[...] = dot_nt(w_down[:, mine], token_rows(own))


def backward_kernel(
    where, own_part, other, gate, up, w_gate, w_up, w_down, send, grad_gate, grad_up
):
    _, theirs = halves(where, 2 * other.shape[3])
    grad_hidden = own_part[...] + dot_nt(w_down[:, theirs], token_rows(other))
    gate_pre = gate[...]
    to_gate = (grad_hidden * up[...] * gelu_slope(gate_pre)).T.astype(BF16)
    to_up = (grad_hidden * gelu_tanh(gate_pre)).T.astype(BF16)
    grad_gate[...] = to_gate
    grad_up[...] = to_up
    send[...] = (dot_nn(to_gate, w_gate[:, theirs]) + dot_nn(to_up, w_up[:, theirs])).astype(BF16)


def backward_own_kernel(where, grad_gate, grad_up, w_gate, w_up, out):
    mine, _ = halves(where, out.shape[1])
    out[...] = dot_nn(grad_gate[...], w_gate[:, mine]) + dot_nn(grad_up[...], w_up[:, mine])


def input_kernel(where, own, other, stream, grad_output, gains, out, whole):
    rows = stream[...]
    inv_pre = lax.rsqrt(mean_row(rows * rows) + epsilon)
    pre_grad = gains[0:1] * joined(where, own, other, whole)
    whole[...] = (
        grad_output[...]
        + inv_pre * pre_grad
        - rows * (inv_pre * inv_pre * inv_pre) * mean_row(pre_grad * rows)
    )
    spread_quarters(where, whole, out)


def code_of(where, own, other, w_enc, b_enc):
    first, second = halves(where, own.shape[1])
    return jax.nn.relu(
        dot_nn(own[...], w_enc[first, :]) + dot_nn(other[...], w_enc[second, :]) + b_enc[...]
    )


def code_kernel(where, own, other, w_enc, b_enc, out):
    out[...] = code_of(where, own, other, w_enc, b_enc)


def change_kernel(where, own, other, w_enc, b_enc, clean_code, out):
    out[...] = clean_code[...] - code_of(where, own, other, w_enc, b_enc)


def attribution_own_kernel(where, own, w_dec, out):
    mine, _ = halves(where, 2 * own.shape[3])
    out[...] = dot_nt(w_dec[:, mine], token_rows(own))


def attribution_kernel(where, part, other, w_dec, change, out):
    _, theirs = halves(where, 2 * other.shape[3])
    projected = part[...] + dot_nt(w_dec[:, theirs], token_rows(other))
    out[...] = jnp.sum(change[...] * projected.T, axis=0, keepdims=True)


def exchanged_by_core(blocks):
    flat = blocks.reshape(-1, *blocks.shape[2:])
    return lax.all_to_all(flat, CORES, 0, 0, tiled=True).reshape(blocks.shape)


def swapped(value):
    return lax.ppermute(value, "core", SWAP)


def local(
    resid_clean,
    resid_corrupt,
    answer_ids,
    unembed,
    pre_gain,
    post_gain,
    final_gain,
    w_gate,
    w_up,
    w_down,
    w_enc,
    b_enc,
    w_dec,
):
    width = resid_clean.shape[1]
    half = width // 2
    chips, plane = lax.axis_size(CHIPS), lax.axis_size(("x", "z"))
    tokens = 2 * chips
    core_index = lax.axis_index("core")
    pair = (
        lax.axis_index("y_lo") * (4 * plane)
        + lax.axis_index("y_hi") * plane
        + lax.axis_index(("x", "z"))
    )
    where = jnp.stack([core_index, pair, pair + 2 * plane]).astype(jnp.int32)
    hidden_units, latents = w_gate.shape[1], w_enc.shape[1]
    w_gate, w_up = w_gate.T, w_up.T
    b_enc = b_enc[None]

    halved = shape((tokens, half), BF16)
    halved32 = shape((tokens, half), F32)
    pairs = shape((chips, 2, 2, half // 2), BF16)
    pair_rows = shape((2, width), F32)
    pair_half = shape((2, half), F32)
    units = shape((tokens, hidden_units), BF16)
    units32 = shape((hidden_units, tokens), F32)
    codes = shape((tokens, latents), F32)
    whole = pltpu.VMEM((2, width), F32)

    partner = (swapped(resid_clean), swapped(resid_corrupt))
    one_row = shape((1, width), BF16)
    held = call(
        load_kernel,
        (one_row, one_row),
        resid_clean, resid_corrupt,
        source=pltpu.HBM,
        scratch=[pltpu.SemaphoreType.DMA((2,))],
    )
    *partner, where, clean, corrupt = lax.optimization_barrier((*partner, where, *held))
    quads, stream = call(
        chip_rows_kernel,
        (shape((chips, 2, 4, half // 2), BF16), pair_rows),
        where, clean, corrupt, *partner,
        scratch=[pltpu.VMEM((4, width), F32)],
        flops=HINT,
    )
    own, own_corrupt = call(
        rows_kernel,
        (halved, halved),
        exchanged_by_core(quads), w_enc, w_gate, w_up, w_down, unembed, pre_gain, post_gain, final_gain,
        flops=HINT,
    )
    pre_gain, own_corrupt = lax.optimization_barrier((pre_gain, own_corrupt))
    gains = call(gains_kernel, shape((3, width), F32), pre_gain, post_gain, final_gain)
    weighted = call(wanted_kernel, pair_rows, where, answer_ids.T, unembed, gains)
    other = swapped(own)
    other, own_corrupt, gains, weighted = lax.optimization_barrier(
        (other, own_corrupt, gains, weighted)
    )
    other_corrupt = swapped(own_corrupt)

    sent, hidden, gate, up = call(
        forward_kernel,
        (halved, units, units32, units32),
        where, own, other, w_gate, w_up, w_down, gains,
    )
    sent, other_corrupt = lax.optimization_barrier((sent, other_corrupt))
    arrived = swapped(sent)
    own_sum = call(forward_own_kernel, halved32, where, hidden, w_down)
    arrived, own_sum = lax.optimization_barrier((arrived, own_sum))
    own_mlp = call(
        total_kernel, pair_half, exchanged_by_core(call(chip_sum_kernel, pairs, own_sum, arrived))
    )
    own_mlp, own = lax.optimization_barrier((own_mlp, own))
    other_mlp = swapped(own_mlp)
    clean_code = call(code_kernel, codes, where, own, other, w_enc, b_enc)
    other_mlp, clean_code = lax.optimization_barrier((other_mlp, clean_code))
    spread_grad, grad_output = call(
        output_kernel,
        (pairs, pair_rows),
        where, own_mlp, other_mlp, stream, weighted, gains,
        scratch=[whole],
    )

    grad_own = exchanged_by_core(spread_grad)
    grad_other = swapped(grad_own)
    own_part = call(backward_own_half_kernel, units32, where, grad_own, w_down)
    grad_other, own_part = lax.optimization_barrier((grad_other, own_part))
    sent, grad_gate, grad_up = call(
        backward_kernel,
        (halved, units, units),
        where, own_part, grad_other, gate, up, w_gate, w_up, w_down,
    )
    arrived = swapped(sent)
    own_sum = call(backward_own_kernel, halved32, where, grad_gate, grad_up, w_gate, w_up)
    arrived, own_sum = lax.optimization_barrier((arrived, own_sum))
    own_normed = call(
        total_kernel, pair_half, exchanged_by_core(call(chip_sum_kernel, pairs, own_sum, arrived))
    )
    own_normed, own_corrupt = lax.optimization_barrier((own_normed, own_corrupt))
    other_normed = swapped(own_normed)
    change = call(
        change_kernel, codes, where, own_corrupt, other_corrupt, w_enc, b_enc, clean_code
    )
    other_normed, change = lax.optimization_barrier((other_normed, change))
    spread_stream = call(
        input_kernel,
        pairs,
        where, own_normed, other_normed, stream, grad_output, gains,
        scratch=[whole],
    )

    last_own = exchanged_by_core(spread_stream)
    last_other = swapped(last_own)
    own_part = call(
        attribution_own_kernel, shape((latents, tokens), F32), where, last_own, w_dec
    )
    last_other, own_part = lax.optimization_barrier((last_other, own_part))
    return call(
        attribution_kernel,
        shape((1, latents), F32),
        where, own_part, last_other, w_dec, change,
        space=jax.ShapeDtypeStruct,
    )


def solution(mesh):
    fine = Mesh(mesh.devices.reshape(2, 2, 2, 4, 4), DEVICES)
    return jax.shard_map(
        local,
        mesh=fine,
        in_specs=(
            P(DEVICES, None),
            P(DEVICES, None),
            P(),
            P(),
            P(),
            P(),
            P(),
            P(None, DEVICES),
            P(None, DEVICES),
            P(DEVICES, None),
            P(None, DEVICES),
            P(DEVICES),
            P(DEVICES, None),
        ),
        out_specs=P(None, DEVICES),
        check_vma=False,
    )
```
